512 devices in a mesh: pop: 8 (over z_hi, x), blk: 64 (over z_lo, y, core).
Axes of the slice: x: 4, y: 4, z: 16 (z_hi: 2, z_lo: 8; z = z_hi * 8 + z_lo), core: 2. Of those that a mesh axis runs over, the one named last changes fastest.
Arguments:
- v_init: float32 [512, 2, 16384], P('pop', None, 'blk'), may hold values from -6 to 6
- a_init: float32 [512, 2, 16384], P('pop', None, 'blk'), may hold values from 0 to 1
- z_init: bfloat16 [512, 2, 16384], P('pop', None, 'blk'), may hold values from 0 to 1
- base_weight: bfloat16 [16384, 16384], P('blk', 'pop'), may hold values from -0.046875 to 0.046875
- factor_u: bfloat16 [512, 4, 16384], P('pop', None, 'blk'), may hold values from -6 to 6
- factor_v: bfloat16 [512, 4, 16384], P('pop', None, 'blk'), may hold values from -0.046875 to 0.046875
- in_weight: bfloat16 [700, 16384], P(None, 'blk'), may hold values from -0.21875 to 0.21875
- spikes_in: int32 [2, 2, 700], replicated, may hold values 0 or 1
- step_count: int32 [512, 2], P('pop'), may hold values from 1 to 2, as said below
- member_ids: int32 [512], P('pop'), may hold values from 0 to 511, each once
- decay_mem: float32 [16384], P('blk'), may hold values from 0.3 to 0.9
- decay_adapt: float32 [16384], P('blk'), may hold values from 0.5 to 0.95
- thr_base: float32 [16384], P('blk'), may hold values from 0.2 to 1
- thr_adapt: float32 [16384], P('blk'), may hold values from 0.5 to 2
Outputs:
- v_out: float32 [512, 2, 16384], P('pop', None, 'blk')
- a_out: float32 [512, 2, 16384], P('pop', None, 'blk')
The draws below stay inside these ranges and needn't reach their ends.
Inputs may be any that keep to these rules, and one draw needn't show every extreme that they name: `member_ids`: each member appears in exactly one slot. `step_count`: a trial's state stops changing after its last step.
All inputs are finite; a program needn't handle non-finite values.
Results may differ from the reference program's by a relative error of at most 0.00088.
Values may be sent and summed in bfloat16 or wider, within the bound.
No kernel may reach another device: no remote copies, remote signals or barrier semaphores. Data moves between devices by JAX's collectives and lax.ppermute only.
A program may use at most 64 MiB of HBM per device.

```python
import jax
import jax.numpy as jnp
from jax import lax

N = 16384
N_IN = 700
RANK = 4
STEPS = 2
TRIALS = 2
MEMBERS = 512


def draw_step_count(key, part):
    counts = jax.random.randint(key, (MEMBERS * TRIALS,), 1, STEPS + 1)
    counts = counts.at[0].set(STEPS)
    counts = counts.at[MEMBERS * TRIALS - 1].set(1)
    return counts.reshape(MEMBERS, TRIALS).astype(jnp.int32)


def place_ends(entries, stream_key, low, top_value):
    longest = entries.shape.index(max(entries.shape))
    spots = []
    for shift in (0, 1):
        where = [jax.random.randint(jax.random.fold_in(stream_key, axis), (), 0, length) for axis, length in enumerate(entries.shape)]
        where[longest] = (where[longest] + shift) % entries.shape[longest]
        spots.append(tuple(where))
    return entries.at[spots[0]].set(low).at[spots[1]].set(top_value)


def shard_levels(stream_key, shape, pieces, least, high):
    def one(axis_at, blocks):
        steps = jax.random.uniform(jax.random.fold_in(jax.random.fold_in(stream_key, 6), axis_at), (blocks,), jnp.float32, least / len(pieces), high / len(pieces))
        return jnp.repeat(jnp.exp(steps), shape[axis_at] // blocks).reshape((-1,) + (1,) * (len(shape) - axis_at - 1))

    gain = one(*pieces[0])
    for cut in pieces[1:]:
        gain = gain * one(*cut)
    return gain


def centred(rng, extent, spread, most, cuts=(), held_as=jnp.bfloat16):
    values = jax.random.normal(rng, extent, jnp.float32) * spread
    if len(cuts) > 0:
        values = shard_levels(rng, extent, cuts, -0.22, 0.18) * values
    return jnp.clip(values, min=-most, max=most).astype(held_as)


def setup_inputs(seed: int = 0) -> dict:
    arg_keys = jax.random.split(jax.random.key(seed), 15)
    v_init = centred(arg_keys[0], (MEMBERS, TRIALS, N), 1.0, 6.0, ((0, 8), (2, 64)), jnp.float32)
    a_init = jnp.clip(1.0 * jax.random.uniform(arg_keys[1], (MEMBERS, TRIALS, N), jnp.float32) ** shard_levels(arg_keys[1], (MEMBERS, TRIALS, N), ((0, 8), (2, 64)), -0.2, 0.2), 0.0, 1.0)
    z_init = jnp.clip(1.0 * jax.random.uniform(arg_keys[2], (MEMBERS, TRIALS, N), jnp.float32) ** shard_levels(arg_keys[2], (MEMBERS, TRIALS, N), ((0, 8), (2, 64)), -0.2, 0.2), 0.0, 1.0).astype(jnp.bfloat16)
    base_weight = centred(arg_keys[3], (N, N), N ** -0.5, 0.046875, ((0, 64), (1, 8)))
    factor_u = centred(arg_keys[4], (MEMBERS, RANK, N), 1.0, 6.0, ((0, 8), (2, 64)))
    factor_v = centred(arg_keys[5], (MEMBERS, RANK, N), N ** -0.5, 0.046875, ((0, 8), (2, 64)))
    in_weight = centred(arg_keys[6], (N_IN, N), N_IN ** -0.5, 0.21875, ((1, 64),))
    spikes_in = place_ends((jax.random.randint(arg_keys[7], (STEPS, TRIALS, N_IN), 0, 2) < 1).astype(jnp.int32), jax.random.fold_in(arg_keys[7], 1), 0, 1)
    step_count = draw_step_count(jax.random.fold_in(arg_keys[14], 71), 0)
    member_ids = jax.random.permutation(arg_keys[9], MEMBERS).astype(jnp.int32)
    decay_mem = jnp.clip(0.3 + 0.59999996 * jax.random.uniform(arg_keys[10], (N,), jnp.float32) ** shard_levels(arg_keys[10], (N,), ((0, 64),), -0.2, 0.2), 0.3, 0.9)
    decay_adapt = jnp.clip(0.5 + 0.45 * jax.random.uniform(arg_keys[11], (N,), jnp.float32) ** shard_levels(arg_keys[11], (N,), ((0, 64),), -0.2, 0.2), 0.5, 0.95)
    thr_base = jnp.clip(0.2 + 0.8 * jax.random.uniform(arg_keys[12], (N,), jnp.float32) ** shard_levels(arg_keys[12], (N,), ((0, 64),), -0.2, 0.2), 0.2, 1.0)
    thr_adapt = jnp.clip(0.5 + 1.5 * jax.random.uniform(arg_keys[13], (N,), jnp.float32) ** shard_levels(arg_keys[13], (N,), ((0, 64),), -0.2, 0.2), 0.5, 2.0)
    return dict(v_init=v_init, a_init=a_init, z_init=z_init, base_weight=base_weight, factor_u=factor_u, factor_v=factor_v, in_weight=in_weight, spikes_in=spikes_in, step_count=step_count, member_ids=member_ids, decay_mem=decay_mem, decay_adapt=decay_adapt, thr_base=thr_base, thr_adapt=thr_adapt)


def reference(v_init, a_init, z_init, base_weight, factor_u, factor_v, in_weight, spikes_in, step_count, member_ids, decay_mem, decay_adapt, thr_base, thr_adapt):
    sign = (1 - 2 * (member_ids % 2)).astype(jnp.float32)
    factor_uf = factor_u.astype(jnp.float32)
    factor_vf = factor_v.astype(jnp.float32)
    state_v, state_a, spikes = v_init, a_init, z_init
    for step in range(STEPS):
        spikes_f = spikes.astype(jnp.float32)
        proj = jnp.einsum("mtn,mkn->mtk", spikes_f, factor_vf).astype(jnp.bfloat16)
        low = jnp.einsum("mtk,mkn->mtn", proj.astype(jnp.float32), factor_uf)
        dense = lax.dot_general(spikes.reshape(-1, N), base_weight, (((1,), (1,)), ((), ())), preferred_element_type=jnp.float32).reshape(spikes.shape)
        current = jnp.dot(spikes_in[step].astype(jnp.bfloat16), in_weight, preferred_element_type=jnp.float32)
        drive = dense + 0.5 * sign[:, None, None] * low + current[None]
        v_new = decay_mem * state_v + (1.0 - decay_mem) * drive - spikes_f * (thr_base + thr_adapt * state_a)
        a_new = decay_adapt * state_a + (1.0 - decay_adapt) * spikes_f
        active = (step_count > step)[:, :, None]
        state_v = jnp.where(active, v_new, state_v)
        state_a = jnp.where(active, a_new, state_a)
        if step + 1 < STEPS:
            spikes = jax.nn.sigmoid(3.0 * (state_v - thr_base - thr_adapt * state_a)).astype(jnp.bfloat16)
    return state_v, state_a
```

```python
import functools

import jax
import jax.numpy as jnp
import numpy as np
from jax import lax
from jax.experimental import pallas as pl
from jax.experimental.pallas import tpu as pltpu
from jax.sharding import Mesh
from jax.sharding import PartitionSpec as P

STEPS = 2
AXES = ("zh", "x", "a", "b", "y", "c")
SIZES = (2, 4, 2, 4, 4, 2)
POP = ("zh", "x")
BLK = ("a", "b", "y", "c")
EXT = 8


def permute(value, dest):
    pairs = []
    for source in np.ndindex(*SIZES):
        there = dest(*source)
        pairs.append(
            (int(np.ravel_multi_index(source, SIZES)), int(np.ravel_multi_index(there, SIZES)))
        )
    return lax.ppermute(value, AXES, pairs)


def to_owner(value):
    return permute(value, lambda zh, x, a, b, y, c: (a, b, zh, x ^ b, y, c))


def over_a(value):
    return permute(value, lambda zh, x, a, b, y, c: (zh, x, 1 - a, b, y, c))


def over_b(value, k):
    return permute(value, lambda zh, x, a, b, y, c: (zh, x, a, b ^ k, y, c))


def over_y(value, k):
    return permute(value, lambda zh, x, a, b, y, c: (zh, x, a, b, y ^ k, c))


def over_c(value):
    return permute(value, lambda zh, x, a, b, y, c: (zh, x, a, b, y, 1 - c))


def over_x(value, k):
    return permute(value, lambda zh, x, a, b, y, c: (zh, x ^ k, a, b, y, c))


def over_zh(value):
    return permute(value, lambda zh, x, a, b, y, c: (1 - zh, x, a, b, y, c))


def member_mask(rows, cols, trials, rank):
    row = lax.broadcasted_iota(jnp.int32, (rows, cols), 0) // trials
    col = lax.broadcasted_iota(jnp.int32, (rows, cols), 1) // rank
    return row == col


def pack(spike_rows, factor_rows, trials, rank):
    rows, block = spike_rows.shape
    full = lax.dot_general(
        spike_rows, factor_rows, (((1,), (1,)), ((), ())), preferred_element_type=jnp.float32
    )
    kept = jnp.where(member_mask(rows, full.shape[1], trials, rank), full, 0.0)
    part = kept.reshape(rows // trials, trials, full.shape[1]).sum(0)
    high = lax.reduce_precision(part, 8, 7)
    rest = part - high
    middle = lax.reduce_precision(rest, 8, 7)
    last = rest - middle
    terms = [t.astype(jnp.bfloat16) for t in (high, middle, last)]
    pad = jnp.zeros((EXT - 3 * trials, block), jnp.bfloat16)
    return jnp.concatenate([spike_rows, *terms, pad], axis=0)


def mix_kernel(which_ref, *refs, rows, trials, block):
    chunks, w_ref, out_ref = refs[:-2], refs[-2], refs[-1]
    total = None
    extra = None
    for k, chunk in enumerate(chunks):
        column = pl.multiple_of(which_ref[k] * block, block)
        piece = lax.dot_general(
            chunk[0],
            w_ref[:, pl.ds(column, block)],
            (((1,), (1,)), ((), ())),
            preferred_element_type=jnp.float32,
        )
        tail = chunk[0, rows:, :].astype(jnp.float32)
        total = piece if total is None else total + piece
        extra = tail if extra is None else extra + tail
    out_ref[0] = total
    part = extra[:trials] + extra[trials : 2 * trials] + extra[2 * trials : 3 * trials]
    out_ref[0, rows : rows + trials, :] = part


def mix(which, chunks, weight, rows, trials):
    blocks, tall, block = chunks[0].shape
    spec = pl.BlockSpec((1, tall, block), lambda i, which: (i, 0, 0))
    flops = 2 * blocks * tall * block * block * len(chunks)
    moved = len(chunks) * blocks * tall * block * 2 + weight.size * 2 + blocks * tall * block * 4
    return pl.pallas_call(
        functools.partial(mix_kernel, rows=rows, trials=trials, block=block),
        out_shape=jax.ShapeDtypeStruct((blocks, tall, weight.shape[0]), jnp.float32),
        grid_spec=pltpu.PrefetchScalarGridSpec(
            num_scalar_prefetch=1,
            grid=(blocks,),
            in_specs=[spec] * len(chunks) + [pl.BlockSpec(weight.shape, lambda i, which: (0, 0))],
            out_specs=pl.BlockSpec((1, tall, weight.shape[0]), lambda i, which: (i, 0, 0)),
        ),
        cost_estimate=pl.CostEstimate(flops=flops, bytes_accessed=moved, transcendentals=0),
        name="mix",
    )(which, *chunks, weight)


def body(
    v_init,
    a_init,
    z_init,
    base_weight,
    factor_u,
    factor_v,
    in_weight,
    spikes_in,
    step_count,
    member_ids,
    decay_mem,
    decay_adapt,
    thr_base,
    thr_adapt,
):
    members, trials, block = v_init.shape
    rank = factor_u.shape[1]
    rows = members * trials
    tall = rows + EXT
    at = {name: lax.axis_index(name) for name in AXES}
    sign = (1 - 2 * (member_ids % 2)).astype(jnp.float32)
    u_rows = factor_u.reshape(members * rank, block)
    v_rows = factor_v.reshape(members * rank, block)
    which = jnp.stack([(at["y"] ^ k) * 2 + (at["c"] ^ l) for l in range(2) for k in range(4)])
    state_v, state_a, spikes = (v_init, a_init, z_init)
    for step in range(STEPS):
        spikes_f = spikes.astype(jnp.float32)
        held = to_owner(pack(spikes.reshape(rows, block), v_rows, trials, rank))
        held = held[None]
        for axis, bit, move in (
            ("a", 0, over_a),
            ("b", 1, functools.partial(over_b, k=2)),
            ("b", 0, functools.partial(over_b, k=1)),
        ):
            other = move(held)
            late = ((at[axis] >> bit) & 1) == 1
            held = jnp.concatenate(
                [jnp.where(late, other, held), jnp.where(late, held, other)], axis=0
            )
        near = [held] + [over_y(held, k) for k in (1, 2, 3)]
        far = [over_c(n) for n in near]
        part = mix(which, near + far, base_weight, rows, trials)
        part = part.reshape(2, 2, 2, tall, block)
        mine = part[0, 0]
        for k in (1, 2, 3):
            mine = mine + over_x(part[k & 1, k >> 1], k)
        up = at["zh"] == 1
        total = jnp.where(up, mine[1], mine[0]) + over_zh(jnp.where(up, mine[0], mine[1]))
        proj = total[rows : rows + trials].astype(jnp.bfloat16)
        mask = member_mask(rows, members * rank, trials, rank)
        spread = jnp.broadcast_to(proj[None], (members, trials, members * rank))
        spread = jnp.where(mask, spread.reshape(rows, members * rank), 0).astype(jnp.bfloat16)
        low = lax.dot_general(
            spread, u_rows, (((1,), (0,)), ((), ())), preferred_element_type=jnp.float32
        ).reshape(members, trials, block)
        dense = total[:rows].reshape(members, trials, block)
        current = jnp.dot(
            spikes_in[step].astype(jnp.bfloat16), in_weight, preferred_element_type=jnp.float32
        )
        drive = dense + 0.5 * sign[:, None, None] * low + current[None]
        v_new = (
            decay_mem * state_v
            + (1.0 - decay_mem) * drive
            - spikes_f * (thr_base + thr_adapt * state_a)
        )
        a_new = decay_adapt * state_a + (1.0 - decay_adapt) * spikes_f
        active = (step_count > step)[:, :, None]
        state_v = jnp.where(active, v_new, state_v)
        state_a = jnp.where(active, a_new, state_a)
        if step + 1 < STEPS:
            spikes = jax.nn.sigmoid(3.0 * (state_v - thr_base - thr_adapt * state_a)).astype(
                jnp.bfloat16
            )
    return (state_v, state_a)


def solution(mesh):
    fine = Mesh(mesh.devices.reshape(SIZES), AXES)
    in_specs = (
        P(POP, None, BLK),
        P(POP, None, BLK),
        P(POP, None, BLK),
        P(BLK, POP),
        P(POP, None, BLK),
        P(POP, None, BLK),
        P(None, BLK),
        P(),
        P(POP, None),
        P(POP),
        P(BLK),
        P(BLK),
        P(BLK),
        P(BLK),
    )
    out_specs = (P(POP, None, BLK), P(POP, None, BLK))
    return jax.shard_map(body, mesh=fine, in_specs=in_specs, out_specs=out_specs, check_vma=False)
```

```python
import functools

import jax
import jax.numpy as jnp
import numpy as np
from jax import lax
from jax.experimental import pallas as pl
from jax.experimental.pallas import tpu as pltpu
from jax.sharding import Mesh
from jax.sharding import PartitionSpec as P

STEPS = 2
AXES = ("zh", "x", "a", "b", "y", "c")
SIZES = (2, 4, 2, 4, 4, 2)
POP = ("zh", "x")
BLK = ("a", "b", "y", "c")
EXT = 8


def permute(value, dest):
    pairs = []
    for source in np.ndindex(*SIZES):
        there = dest(*source)
        pairs.append(
            (int(np.ravel_multi_index(source, SIZES)), int(np.ravel_multi_index(there, SIZES)))
        )
    return lax.ppermute(value, AXES, pairs)


def to_owner(value):
    return permute(value, lambda zh, x, a, b, y, c: (a, x, zh, b, y, c))


def over_a(value):
    return permute(value, lambda zh, x, a, b, y, c: (zh, x, 1 - a, b, y, c))


def over_b(value, k):
    return permute(value, lambda zh, x, a, b, y, c: (zh, x, a, b ^ k, y, c))


def over_y(value, k):
    return permute(value, lambda zh, x, a, b, y, c: (zh, x, a, b, y ^ k, c))


def over_c(value):
    return permute(value, lambda zh, x, a, b, y, c: (zh, x, a, b, y, 1 - c))


def over_x(value, k):
    return permute(value, lambda zh, x, a, b, y, c: (zh, x ^ k, a, b, y, c))


def over_zh(value):
    return permute(value, lambda zh, x, a, b, y, c: (1 - zh, x, a, b, y, c))


def member_mask(rows, cols, trials, rank):
    row = lax.broadcasted_iota(jnp.int32, (rows, cols), 0) // trials
    col = lax.broadcasted_iota(jnp.int32, (rows, cols), 1) // rank
    return row == col


def pack(spike_rows, factor_rows, trials, rank):
    rows, block = spike_rows.shape
    full = lax.dot_general(
        spike_rows, factor_rows, (((1,), (1,)), ((), ())), preferred_element_type=jnp.float32
    )
    kept = jnp.where(member_mask(rows, full.shape[1], trials, rank), full, 0.0)
    part = kept.reshape(rows // trials, trials, full.shape[1]).sum(0)
    high = lax.reduce_precision(part, 8, 7)
    rest = part - high
    middle = lax.reduce_precision(rest, 8, 7)
    last = rest - middle
    terms = [t.astype(jnp.bfloat16) for t in (high, middle, last)]
    pad = jnp.zeros((EXT - 3 * trials, block), jnp.bfloat16)
    return jnp.concatenate([spike_rows, *terms, pad], axis=0)


def mix_kernel(at_ref, *refs, rows, trials):
    spikes, weights, mine_ref, theirs_ref = refs[:4], refs[4:8], refs[8], refs[9]
    flip, shift, y = at_ref[0], at_ref[1], at_ref[2]
    tall, block = spikes[0].shape[1:]
    total = None
    extra = None
    for q in range(4):
        for k in range(4):
            there = shift ^ k
            first = (there & 1) * 4 + (there >> 1) * 2
            chunk = spikes[q][pl.ds(first, 2)]
            piece = jnp.dot(
                chunk.reshape(2 * tall, block),
                weights[k][y ^ q],
                preferred_element_type=jnp.float32,
            )
            tail = chunk[:, rows:, :].astype(jnp.float32)
            total = piece if total is None else total + piece
            extra = tail if extra is None else extra + tail
    part = extra[:, :trials] + extra[:, trials : 2 * trials] + extra[:, 2 * trials : 3 * trials]
    for s in range(2):
        for half, ref in enumerate((mine_ref, theirs_ref)):
            ref[s ^ flip] = total[s * tall : (s + 1) * tall, half * block : (half + 1) * block]
            ref[s ^ flip, rows : rows + trials, :] = part[s]


def mix(at, spikes, weights, rows, trials):
    blocks, tall, block = spikes[0].shape
    out = jax.ShapeDtypeStruct((2, tall, block), jnp.float32)
    whole = pl.BlockSpec(memory_space=pltpu.VMEM)
    inputs = len(spikes) * spikes[0].size + len(weights) * weights[0].size
    return pl.pallas_call(
        functools.partial(mix_kernel, rows=rows, trials=trials),
        out_shape=(out, out),
        in_specs=[pl.BlockSpec(memory_space=pltpu.SMEM)] + [whole] * 8,
        out_specs=(whole, whole),
        cost_estimate=pl.CostEstimate(
            flops=8 * tall * len(weights) * weights[0].size,
            bytes_accessed=2 * inputs + 16 * tall * block,
            transcendentals=0,
        ),
        name="mix",
    )(at, *spikes, *weights)


def spread_weights(base_weight, at):
    outs, depth = base_weight.shape
    block = depth // 8
    split = base_weight.reshape(outs, 4, 2, block)
    one = at["c"] == 1
    keep = jnp.where(one, split[:, :, 1], split[:, :, 0]).transpose(1, 2, 0)
    give = jnp.where(one, split[:, :, 0], split[:, :, 1]).transpose(1, 2, 0)
    own = jnp.concatenate([keep, over_c(give)], axis=2)
    return [own] + [over_x(own, k) for k in (1, 2, 3)]


def body(
    v_init,
    a_init,
    z_init,
    base_weight,
    factor_u,
    factor_v,
    in_weight,
    spikes_in,
    step_count,
    member_ids,
    decay_mem,
    decay_adapt,
    thr_base,
    thr_adapt,
):
    members, trials, block = v_init.shape
    rank = factor_u.shape[1]
    rows = members * trials
    tall = rows + EXT
    at = {name: lax.axis_index(name) for name in AXES}
    sign = (1 - 2 * (member_ids % 2)).astype(jnp.float32)
    u_rows = factor_u.reshape(members * rank, block)
    v_rows = factor_v.reshape(members * rank, block)
    place = jnp.stack([at["a"] ^ at["zh"], at["b"] ^ at["x"], at["y"]])
    weights = spread_weights(base_weight, at)
    state_v, state_a, spikes = (v_init, a_init, z_init)
    for step in range(STEPS):
        spikes_f = spikes.astype(jnp.float32)
        held = to_owner(pack(spikes.reshape(rows, block), v_rows, trials, rank))
        held = held[None]
        for move in (over_a, functools.partial(over_b, k=2), functools.partial(over_b, k=1)):
            held = jnp.concatenate([held, move(held)], axis=0)
        near = [held] + [over_y(held, k) for k in (1, 2, 3)]
        mine, theirs = mix(place, near, weights, rows, trials)
        mine = mine + over_c(theirs)
        total = mine[0] + over_zh(mine[1])
        proj = total[rows : rows + trials].astype(jnp.bfloat16)
        mask = member_mask(rows, members * rank, trials, rank)
        spread = jnp.broadcast_to(proj[None], (members, trials, members * rank))
        spread = jnp.where(mask, spread.reshape(rows, members * rank), 0).astype(jnp.bfloat16)
        low = lax.dot_general(
            spread, u_rows, (((1,), (0,)), ((), ())), preferred_element_type=jnp.float32
        ).reshape(members, trials, block)
        dense = total[:rows].reshape(members, trials, block)
        current = jnp.dot(
            spikes_in[step].astype(jnp.bfloat16), in_weight, preferred_element_type=jnp.float32
        )
        drive = dense + 0.5 * sign[:, None, None] * low + current[None]
        v_new = (
            decay_mem * state_v
            + (1.0 - decay_mem) * drive
            - spikes_f * (thr_base + thr_adapt * state_a)
        )
        a_new = decay_adapt * state_a + (1.0 - decay_adapt) * spikes_f
        active = (step_count > step)[:, :, None]
        state_v = jnp.where(active, v_new, state_v)
        state_a = jnp.where(active, a_new, state_a)
        if step + 1 < STEPS:
            spikes = jax.nn.sigmoid(3.0 * (state_v - thr_base - thr_adapt * state_a)).astype(
                jnp.bfloat16
            )
    return (state_v, state_a)


def solution(mesh):
    fine = Mesh(mesh.devices.reshape(SIZES), AXES)
    in_specs = (
        P(POP, None, BLK),
        P(POP, None, BLK),
        P(POP, None, BLK),
        P(BLK, POP),
        P(POP, None, BLK),
        P(POP, None, BLK),
        P(None, BLK),
        P(),
        P(POP, None),
        P(POP),
        P(BLK),
        P(BLK),
        P(BLK),
        P(BLK),
    )
    out_specs = (P(POP, None, BLK), P(POP, None, BLK))
    return jax.shard_map(body, mesh=fine, in_specs=in_specs, out_specs=out_specs, check_vma=False)
```

```python
import functools

import jax
import jax.numpy as jnp
import numpy as np
from jax import lax
from jax.experimental import pallas as pl
from jax.experimental.pallas import tpu as pltpu
from jax.sharding import Mesh
from jax.sharding import PartitionSpec as P

STEPS = 2
AXES = ("zh", "x", "a", "b", "y", "c")
SIZES = (2, 4, 2, 4, 4, 2)
POP = ("zh", "x")
BLK = ("a", "b", "y", "c")
EXT = 8


def permute(value, dest):
    pairs = []
    for source in np.ndindex(*SIZES):
        there = dest(*source)
        pairs.append(
            (int(np.ravel_multi_index(source, SIZES)), int(np.ravel_multi_index(there, SIZES)))
        )
    return lax.ppermute(value, AXES, pairs)


def to_owner(value):
    return permute(value, lambda zh, x, a, b, y, c: (a, x, zh, b, y, c))


def over_a(value):
    return permute(value, lambda zh, x, a, b, y, c: (zh, x, 1 - a, b, y, c))


def over_b(value, k):
    return permute(value, lambda zh, x, a, b, y, c: (zh, x, a, b ^ k, y, c))


def over_y(value, k):
    return permute(value, lambda zh, x, a, b, y, c: (zh, x, a, b, y ^ k, c))


def over_c(value):
    return permute(value, lambda zh, x, a, b, y, c: (zh, x, a, b, y, 1 - c))


def over_x(value, k):
    return permute(value, lambda zh, x, a, b, y, c: (zh, x ^ k, a, b, y, c))


def over_zh(value):
    return permute(value, lambda zh, x, a, b, y, c: (1 - zh, x, a, b, y, c))


def member_mask(rows, cols, trials, rank):
    row = lax.broadcasted_iota(jnp.int32, (rows, cols), 0) // trials
    col = lax.broadcasted_iota(jnp.int32, (rows, cols), 1) // rank
    return row == col


def pack(spike_rows, factor_rows, trials, rank):
    rows, block = spike_rows.shape
    full = lax.dot_general(
        spike_rows, factor_rows, (((1,), (1,)), ((), ())), preferred_element_type=jnp.float32
    )
    kept = jnp.where(member_mask(rows, full.shape[1], trials, rank), full, 0.0)
    part = kept.reshape(rows // trials, trials, full.shape[1]).sum(0)
    high = lax.reduce_precision(part, 8, 7)
    rest = part - high
    middle = lax.reduce_precision(rest, 8, 7)
    last = rest - middle
    terms = [t.astype(jnp.bfloat16) for t in (high, middle, last)]
    pad = jnp.zeros((EXT - 3 * trials, block), jnp.bfloat16)
    return jnp.concatenate([spike_rows, *terms, pad], axis=0)


def mix_kernel(at_ref, *refs, rows, trials, late):
    spikes, weights = refs[:4], refs[4:8]
    mine_ref, theirs_ref = refs[-2:]
    flip, shift, y = at_ref[0], at_ref[1], at_ref[2]
    tall, block = spikes[0].shape[1:]
    extra = None
    for q in range(4):
        tail = spikes[q][:2, rows:, :].astype(jnp.float32)
        tail = tail + spikes[q][2:, rows:, :].astype(jnp.float32)
        extra = tail if extra is None else extra + tail
    part = extra[:, :trials] + extra[:, trials : 2 * trials] + extra[:, 2 * trials : 3 * trials]

    def run(low):
        total = None
        for q in range(4):
            for high in range(2):
                first = ((shift >> 1) ^ high) * 2
                chunk = spikes[q][pl.ds(first, 2)]
                piece = jnp.dot(
                    chunk.reshape(2 * tall, block),
                    weights[2 * high + low][y ^ q],
                    preferred_element_type=jnp.float32,
                )
                total = piece if total is None else total + piece
        for s in range(2):
            for half, ref in enumerate((mine_ref, theirs_ref)):
                value = total[s * tall : (s + 1) * tall, half * block : (half + 1) * block]
                other = part[s]
                if late:
                    before = refs[8 + half]
                    value = value + before[s ^ flip]
                    other = other + before[s ^ flip, rows : rows + trials, :]
                ref[s ^ flip] = value
                ref[s ^ flip, rows : rows + trials, :] = other

    for low in range(2):
        pl.when(((shift & 1) ^ int(late)) == low)(functools.partial(run, low))


def mix(at, spikes, weights, rows, trials, before=()):
    blocks, tall, block = spikes[0].shape
    out = jax.ShapeDtypeStruct((2, tall, block), jnp.float32)
    whole = pl.BlockSpec(memory_space=pltpu.VMEM)
    inputs = len(spikes) * spikes[0].size + 2 * weights[0].size
    return pl.pallas_call(
        functools.partial(mix_kernel, rows=rows, trials=trials, late=len(before) > 0),
        out_shape=(out, out),
        in_specs=[pl.BlockSpec(memory_space=pltpu.SMEM)] + [whole] * (8 + len(before)),
        out_specs=(whole, whole),
        cost_estimate=pl.CostEstimate(
            flops=4 * blocks * tall * weights[0].size // 2,
            bytes_accessed=2 * inputs + 16 * tall * block,
            transcendentals=0,
        ),
        name="mix_late" if before else "mix_early",
    )(at, *spikes, *weights, *before)


def fold_kernel(mine_ref, theirs_ref, keep_ref, give_ref, *, rows, trials):
    keep_ref[...] = mine_ref[0] + theirs_ref[0]
    give = mine_ref[1] + theirs_ref[1]
    tail = give[rows : rows + trials]
    high = tail.astype(jnp.bfloat16).astype(jnp.float32)
    rest = tail - high
    middle = rest.astype(jnp.bfloat16).astype(jnp.float32)
    pad = jnp.zeros((EXT - 3 * trials, tail.shape[1]), jnp.float32)
    sent = jnp.concatenate([give[:rows], high, middle, rest - middle, pad], axis=0)
    give_ref[...] = sent.astype(jnp.bfloat16)


def fold(mine, theirs, rows, trials):
    shape = mine.shape[1:]
    whole = pl.BlockSpec(memory_space=pltpu.VMEM)
    return pl.pallas_call(
        functools.partial(fold_kernel, rows=rows, trials=trials),
        out_shape=(
            jax.ShapeDtypeStruct(shape, jnp.float32),
            jax.ShapeDtypeStruct(shape, jnp.bfloat16),
        ),
        in_specs=[whole, whole],
        out_specs=(whole, whole),
        name="fold",
    )(mine, theirs)


def spread_weights(base_weight, at):
    outs, depth = base_weight.shape
    block = depth // 8
    split = base_weight.reshape(outs, 4, 2, block)
    one = at["c"] == 1
    keep = jnp.where(one, split[:, :, 1], split[:, :, 0]).transpose(1, 2, 0)
    give = jnp.where(one, split[:, :, 0], split[:, :, 1]).transpose(1, 2, 0)
    own = jnp.concatenate([keep, over_c(give)], axis=2)
    chunks = [own]
    for k in (1, 2, 3):
        chunks.append(over_x(own, k))
    return chunks


def body(
    v_init,
    a_init,
    z_init,
    base_weight,
    factor_u,
    factor_v,
    in_weight,
    spikes_in,
    step_count,
    member_ids,
    decay_mem,
    decay_adapt,
    thr_base,
    thr_adapt,
):
    members, trials, block = v_init.shape
    rank = factor_u.shape[1]
    rows = members * trials
    at = {name: lax.axis_index(name) for name in AXES}
    sign = (1 - 2 * (member_ids % 2)).astype(jnp.float32)
    u_rows = factor_u.reshape(members * rank, block)
    v_rows = factor_v.reshape(members * rank, block)
    place = jnp.stack([at["a"] ^ at["zh"], at["b"] ^ at["x"], at["y"]])
    weights = spread_weights(base_weight, at)
    state_v, state_a, spikes = (v_init, a_init, z_init)
    for step in range(STEPS):
        spikes_f = spikes.astype(jnp.float32)
        held = pack(spikes.reshape(rows, block), v_rows, trials, rank)
        held = to_owner(held)[None]
        other = over_a(held)
        held = jnp.concatenate([held, other], axis=0)
        other = over_b(held, 2)
        early = [jnp.concatenate([held, other], axis=0)]
        late = [over_b(early[0], 1)]
        for pieces in (early, late):
            for k in (1, 2, 3):
                pieces.append(over_y(pieces[0], k))
        halves = mix(place, early, weights, rows, trials)
        mine, theirs = mix(place, late, weights, rows, trials, halves)
        theirs = over_c(theirs)
        keep, give = fold(mine, theirs, rows, trials)
        came = over_zh(give).astype(jnp.float32)
        total = keep[:rows] + came[:rows]
        proj = keep[rows : rows + trials]
        for term in range(3):
            proj = proj + came[rows + term * trials : rows + (term + 1) * trials]
        proj = proj.astype(jnp.bfloat16)
        mask = member_mask(rows, members * rank, trials, rank)
        spread = jnp.broadcast_to(proj[None], (members, trials, members * rank))
        spread = jnp.where(mask, spread.reshape(rows, members * rank), 0).astype(jnp.bfloat16)
        low = lax.dot_general(
            spread, u_rows, (((1,), (0,)), ((), ())), preferred_element_type=jnp.float32
        ).reshape(members, trials, block)
        dense = total.reshape(members, trials, block)
        current = jnp.dot(
            spikes_in[step].astype(jnp.bfloat16), in_weight, preferred_element_type=jnp.float32
        )
        drive = dense + 0.5 * sign[:, None, None] * low + current[None]
        v_new = (
            decay_mem * state_v
            + (1.0 - decay_mem) * drive
            - spikes_f * (thr_base + thr_adapt * state_a)
        )
        a_new = decay_adapt * state_a + (1.0 - decay_adapt) * spikes_f
        active = (step_count > step)[:, :, None]
        state_v = jnp.where(active, v_new, state_v)
        state_a = jnp.where(active, a_new, state_a)
        if step + 1 < STEPS:
            spikes = jax.nn.sigmoid(3.0 * (state_v - thr_base - thr_adapt * state_a)).astype(
                jnp.bfloat16
            )
    return (state_v, state_a)


def solution(mesh):
    fine = Mesh(mesh.devices.reshape(SIZES), AXES)
    in_specs = (
        P(POP, None, BLK),
        P(POP, None, BLK),
        P(POP, None, BLK),
        P(BLK, POP),
        P(POP, None, BLK),
        P(POP, None, BLK),
        P(None, BLK),
        P(),
        P(POP, None),
        P(POP),
        P(BLK),
        P(BLK),
        P(BLK),
        P(BLK),
    )
    out_specs = (P(POP, None, BLK), P(POP, None, BLK))
    return jax.shard_map(body, mesh=fine, in_specs=in_specs, out_specs=out_specs, check_vma=False)
```

```python
import functools

import jax
import jax.numpy as jnp
import numpy as np
from jax import lax
from jax.experimental import pallas as pl
from jax.experimental.pallas import tpu as pltpu
from jax.sharding import Mesh
from jax.sharding import PartitionSpec as P

STEPS = 2
AXES = ("zh", "x", "a", "b", "y", "c")
SIZES = (2, 4, 2, 4, 4, 2)
POP = ("zh", "x")
BLK = ("a", "b", "y", "c")
EXT = 8


def permute(value, dest):
    pairs = []
    for source in np.ndindex(*SIZES):
        there = dest(*source)
        pairs.append(
            (int(np.ravel_multi_index(source, SIZES)), int(np.ravel_multi_index(there, SIZES)))
        )
    return lax.ppermute(value, AXES, pairs)


def to_owner(value):
    return permute(value, lambda zh, x, a, b, y, c: (a, x, zh, b, y, c))


def over_a(value):
    return permute(value, lambda zh, x, a, b, y, c: (zh, x, 1 - a, b, y, c))


def over_b(value, k):
    return permute(value, lambda zh, x, a, b, y, c: (zh, x, a, b ^ k, y, c))


def over_y(value, k):
    return permute(value, lambda zh, x, a, b, y, c: (zh, x, a, b, y ^ k, c))


def over_c(value):
    return permute(value, lambda zh, x, a, b, y, c: (zh, x, a, b, y, 1 - c))


def over_x(value, k):
    return permute(value, lambda zh, x, a, b, y, c: (zh, x ^ k, a, b, y, c))


def over_zh(value):
    return permute(value, lambda zh, x, a, b, y, c: (1 - zh, x, a, b, y, c))


def member_mask(rows, cols, trials, rank):
    row = lax.broadcasted_iota(jnp.int32, (rows, cols), 0) // trials
    col = lax.broadcasted_iota(jnp.int32, (rows, cols), 1) // rank
    return row == col


def by_trial(values, rows):
    trials, block = values.shape
    trial = lax.broadcasted_iota(jnp.int32, (rows, block), 0) % trials
    out = jnp.broadcast_to(values[:1], (rows, block))
    for j in range(1, trials):
        out = jnp.where(trial == j, jnp.broadcast_to(values[j : j + 1], (rows, block)), out)
    return out


def three_terms(value):
    high = value.astype(jnp.bfloat16).astype(jnp.float32)
    rest = value - high
    middle = rest.astype(jnp.bfloat16).astype(jnp.float32)
    return [high, middle, rest - middle]


def store_packed(out_ref, spikes, factors, trials, rank):
    rows, block = spikes.shape
    full = lax.dot_general(
        spikes, factors, (((1,), (1,)), ((), ())), preferred_element_type=jnp.float32
    )
    kept = jnp.where(member_mask(rows, full.shape[1], trials, rank), full, 0.0)
    trial = lax.broadcasted_iota(jnp.int32, kept.shape, 0) % trials
    parts = [
        jnp.sum(jnp.where(trial == j, kept, 0.0), axis=0, keepdims=True) for j in range(trials)
    ]
    terms = three_terms(jnp.concatenate(parts, axis=0))
    pad = jnp.zeros((EXT - 3 * trials, block), jnp.float32)
    out_ref[:rows] = spikes
    out_ref[rows:] = jnp.concatenate([*terms, pad], axis=0).astype(jnp.bfloat16)


def pack_kernel(spikes_ref, factors_ref, out_ref, *, trials, rank):
    store_packed(out_ref, spikes_ref[...], factors_ref[...], trials, rank)


def pack(spikes, factors, trials, rank):
    rows, block = spikes.shape
    whole = pl.BlockSpec(memory_space=pltpu.VMEM)
    return pl.pallas_call(
        functools.partial(pack_kernel, trials=trials, rank=rank),
        out_shape=jax.ShapeDtypeStruct((rows + EXT, block), jnp.bfloat16),
        in_specs=[whole] * 2,
        out_specs=whole,
        compiler_params=pltpu.CompilerParams(vmem_limit_bytes=4 << 20),
        name="pack",
    )(spikes, factors)


def update_kernel(
    keep_ref, came_ref, packed_ref, v_ref, a_ref, lanes_ref, cols_ref, u_ref, f_ref, *outs, **sizes
):
    step, trials, rank = sizes["step"], sizes["trials"], sizes["rank"]
    rows, _ = v_ref.shape
    total = keep_ref[:rows] + came_ref[:rows].astype(jnp.float32)
    tail = came_ref[rows:].astype(jnp.float32)
    proj = keep_ref[rows : rows + trials]
    for term in range(3):
        proj = proj + tail[term * trials : (term + 1) * trials]
    mask = member_mask(rows, u_ref.shape[0], trials, rank)
    spread = jnp.where(mask, by_trial(proj, rows), 0.0).astype(jnp.bfloat16)
    low = jnp.dot(spread, u_ref[...], preferred_element_type=jnp.float32)
    current = by_trial(lanes_ref[4 + step * trials : 4 + (step + 1) * trials], rows)
    drive = total + cols_ref[:, :1] * low + current
    decay_mem, decay_adapt = lanes_ref[0:1], lanes_ref[1:2]
    base, adapt = lanes_ref[2:3], lanes_ref[3:4]
    spikes = packed_ref[:rows].astype(jnp.float32)
    v, a = v_ref[...], a_ref[...]
    v_new = decay_mem * v + (1.0 - decay_mem) * drive - spikes * (base + adapt * a)
    a_new = decay_adapt * a + (1.0 - decay_adapt) * spikes
    active = cols_ref[:, 1:2] > float(step)
    v = jnp.where(active, v_new, v)
    a = jnp.where(active, a_new, a)
    outs[0][...] = v
    outs[1][...] = a
    if len(outs) > 2:
        fresh = jax.nn.sigmoid(3.0 * (v - base - adapt * a)).astype(jnp.bfloat16)
        store_packed(outs[2], fresh, f_ref[...], trials, rank)


def update(keep, came, packed, v, a, lanes, cols, u_rows, f_rows, step, trials, rank):
    state = jax.ShapeDtypeStruct(v.shape, jnp.float32)
    outs = [state, state]
    if step + 1 < STEPS:
        outs.append(jax.ShapeDtypeStruct(packed.shape, packed.dtype))
    whole = pl.BlockSpec(memory_space=pltpu.VMEM)
    return pl.pallas_call(
        functools.partial(update_kernel, step=step, trials=trials, rank=rank),
        out_shape=tuple(outs),
        in_specs=[whole] * 9,
        out_specs=(whole,) * len(outs),
        compiler_params=pltpu.CompilerParams(vmem_limit_bytes=6 << 20),
        name="update",
    )(keep, came, packed, v, a, lanes, cols, u_rows, f_rows)


def mix_kernel(at_ref, *refs, rows, trials, late):
    spikes, weights = refs[:4], refs[4:8]
    mine_ref, theirs_ref = refs[-2:]
    flip, shift, y = at_ref[0], at_ref[1], at_ref[2]
    tall, block = spikes[0].shape[1:]
    extra = None
    for q in range(4):
        tail = spikes[q][:2, rows:, :].astype(jnp.float32)
        tail = tail + spikes[q][2:, rows:, :].astype(jnp.float32)
        extra = tail if extra is None else extra + tail
    part = extra[:, :trials] + extra[:, trials : 2 * trials] + extra[:, 2 * trials : 3 * trials]

    def run(low):
        total = None
        for q in range(4):
            for high in range(2):
                first = ((shift >> 1) ^ high) * 2
                chunk = spikes[q][pl.ds(first, 2)]
                piece = jnp.dot(
                    chunk.reshape(2 * tall, block),
                    weights[2 * high + low][y ^ q],
                    preferred_element_type=jnp.float32,
                )
                total = piece if total is None else total + piece
        for s in range(2):
            for half, ref in enumerate((mine_ref, theirs_ref)):
                value = total[s * tall : (s + 1) * tall, half * block : (half + 1) * block]
                other = part[s]
                if late:
                    before = refs[8 + half]
                    value = value + before[s ^ flip]
                    other = other + before[s ^ flip, rows : rows + trials, :]
                ref[s ^ flip] = value
                ref[s ^ flip, rows : rows + trials, :] = other

    for low in range(2):
        pl.when(((shift & 1) ^ int(late)) == low)(functools.partial(run, low))


def mix(at, spikes, weights, rows, trials, before=()):
    blocks, tall, block = spikes[0].shape
    out = jax.ShapeDtypeStruct((2, tall, block), jnp.float32)
    whole = pl.BlockSpec(memory_space=pltpu.VMEM)
    inputs = len(spikes) * spikes[0].size + 2 * weights[0].size
    return pl.pallas_call(
        functools.partial(mix_kernel, rows=rows, trials=trials, late=len(before) > 0),
        out_shape=(out, out),
        in_specs=[pl.BlockSpec(memory_space=pltpu.SMEM)] + [whole] * (8 + len(before)),
        out_specs=(whole, whole),
        cost_estimate=pl.CostEstimate(
            flops=4 * blocks * tall * weights[0].size // 2,
            bytes_accessed=2 * inputs + 16 * tall * block,
            transcendentals=0,
        ),
        compiler_params=pltpu.CompilerParams(vmem_limit_bytes=12 << 20),
        name="mix_late" if before else "mix_early",
    )(at, *spikes, *weights, *before)


def fold_kernel(mine_ref, theirs_ref, keep_ref, give_ref, *, rows, trials):
    keep_ref[...] = mine_ref[0] + theirs_ref[0]
    give = mine_ref[1] + theirs_ref[1]
    terms = three_terms(give[rows : rows + trials])
    pad = jnp.zeros((EXT - 3 * trials, give.shape[1]), jnp.float32)
    give_ref[...] = jnp.concatenate([give[:rows], *terms, pad], axis=0).astype(jnp.bfloat16)


def fold(mine, theirs, rows, trials):
    shape = mine.shape[1:]
    whole = pl.BlockSpec(memory_space=pltpu.VMEM)
    return pl.pallas_call(
        functools.partial(fold_kernel, rows=rows, trials=trials),
        out_shape=(
            jax.ShapeDtypeStruct(shape, jnp.float32),
            jax.ShapeDtypeStruct(shape, jnp.bfloat16),
        ),
        in_specs=[whole, whole],
        out_specs=(whole, whole),
        compiler_params=pltpu.CompilerParams(vmem_limit_bytes=4 << 20),
        name="fold",
    )(mine, theirs)


def spread_weights(base_weight, at):
    outs, depth = base_weight.shape
    block = depth // 8
    split = base_weight.reshape(outs, 4, 2, block)
    one = at["c"] == 1
    keep = jnp.where(one, split[:, :, 1], split[:, :, 0]).transpose(1, 2, 0)
    give = jnp.where(one, split[:, :, 0], split[:, :, 1]).transpose(1, 2, 0)
    got = over_c(give)
    own = jnp.concatenate([keep, got], axis=2)
    chunks = [own]
    for k in (1, 2, 3):
        chunks.append(over_x(own, k))
    return chunks


def body(
    v_init,
    a_init,
    z_init,
    base_weight,
    factor_u,
    factor_v,
    in_weight,
    spikes_in,
    step_count,
    member_ids,
    decay_mem,
    decay_adapt,
    thr_base,
    thr_adapt,
):
    members, trials, block = v_init.shape
    rank = factor_u.shape[1]
    rows = members * trials
    at = {name: lax.axis_index(name) for name in AXES}
    u_rows = factor_u.reshape(members * rank, block)
    f_rows = factor_v.reshape(members * rank, block)
    half_sign = 0.5 * (1 - 2 * (member_ids % 2)).astype(jnp.float32)
    cols = jnp.stack(
        [jnp.repeat(half_sign, trials), step_count.reshape(rows).astype(jnp.float32)], axis=1
    )
    current = jnp.dot(
        spikes_in.reshape(STEPS * trials, -1).astype(jnp.bfloat16),
        in_weight,
        preferred_element_type=jnp.float32,
    )
    lanes = jnp.stack([decay_mem, decay_adapt, thr_base, thr_adapt])
    lanes = jnp.concatenate([lanes, current], axis=0)
    place = jnp.stack([at["a"] ^ at["zh"], at["b"] ^ at["x"], at["y"]])
    v, a = v_init.reshape(rows, block), a_init.reshape(rows, block)
    packed = pack(z_init.reshape(rows, block), f_rows, trials, rank)
    weights = spread_weights(base_weight, at)
    for step in range(STEPS):
        held = to_owner(packed)[None]
        other = over_a(held)
        held = jnp.concatenate([held, other], axis=0)
        other = over_b(held, 2)
        held = jnp.concatenate([held, other], axis=0)
        if step == 0:
            ready = (held, place, lanes, cols, u_rows, v, a)
            held, place, lanes, cols, u_rows, v, a = lax.optimization_barrier(ready)
        early = [held]
        late = [over_b(early[0], 1)]
        for pieces in (early, late):
            for k in (1, 2, 3):
                pieces.append(over_y(pieces[0], k))
        halves = mix(place, early, weights, rows, trials)
        mine, theirs = mix(place, late, weights, rows, trials, halves)
        theirs = over_c(theirs)
        keep, give = fold(mine, theirs, rows, trials)
        came = over_zh(give)
        v, a, *rest = update(
            keep, came, packed, v, a, lanes, cols, u_rows, f_rows, step, trials, rank
        )
        packed = rest[0] if rest else None
    return (v.reshape(v_init.shape), a.reshape(a_init.shape))


def solution(mesh):
    fine = Mesh(mesh.devices.reshape(SIZES), AXES)
    in_specs = (
        P(POP, None, BLK),
        P(POP, None, BLK),
        P(POP, None, BLK),
        P(BLK, POP),
        P(POP, None, BLK),
        P(POP, None, BLK),
        P(None, BLK),
        P(),
        P(POP, None),
        P(POP),
        P(BLK),
        P(BLK),
        P(BLK),
        P(BLK),
    )
    out_specs = (P(POP, None, BLK), P(POP, None, BLK))
    return jax.shard_map(body, mesh=fine, in_specs=in_specs, out_specs=out_specs, check_vma=False)
```

```python
import functools

import jax
import jax.numpy as jnp
import numpy as np
from jax import lax
from jax.experimental import pallas as pl
from jax.experimental.pallas import tpu as pltpu
from jax.sharding import Mesh
from jax.sharding import PartitionSpec as P

STEPS = 2
AXES = ("zh", "x", "a", "b", "y", "c")
SIZES = (2, 4, 2, 4, 4, 2)
POP = ("zh", "x")
BLK = ("a", "b", "y", "c")
EXT = 8


def permute(value, dest):
    pairs = []
    for source in np.ndindex(*SIZES):
        there = dest(*source)
        pairs.append(
            (int(np.ravel_multi_index(source, SIZES)), int(np.ravel_multi_index(there, SIZES)))
        )
    return lax.ppermute(value, AXES, pairs)


def to_owner(value):
    return permute(value, lambda zh, x, a, b, y, c: (a, x, zh, b, y, c))


def over_a(value):
    return permute(value, lambda zh, x, a, b, y, c: (zh, x, 1 - a, b, y, c))


def over_b(value, k):
    return permute(value, lambda zh, x, a, b, y, c: (zh, x, a, b ^ k, y, c))


def over_y(value, k):
    return permute(value, lambda zh, x, a, b, y, c: (zh, x, a, b, y ^ k, c))


def over_c(value):
    return permute(value, lambda zh, x, a, b, y, c: (zh, x, a, b, y, 1 - c))


def over_x(value, k):
    return permute(value, lambda zh, x, a, b, y, c: (zh, x ^ k, a, b, y, c))


def over_zh(value):
    return permute(value, lambda zh, x, a, b, y, c: (1 - zh, x, a, b, y, c))


def member_mask(rows, cols, trials, rank):
    row = lax.broadcasted_iota(jnp.int32, (rows, cols), 0) // trials
    col = lax.broadcasted_iota(jnp.int32, (rows, cols), 1) // rank
    return row == col


def by_trial(values, rows):
    trials, block = values.shape
    trial = lax.broadcasted_iota(jnp.int32, (rows, block), 0) % trials
    out = jnp.broadcast_to(values[:1], (rows, block))
    for j in range(1, trials):
        out = jnp.where(trial == j, jnp.broadcast_to(values[j : j + 1], (rows, block)), out)
    return out


def three_terms(value):
    high = value.astype(jnp.bfloat16).astype(jnp.float32)
    rest = value - high
    middle = rest.astype(jnp.bfloat16).astype(jnp.float32)
    return [high, middle, rest - middle]


def store_packed(out_ref, spikes, factors, trials, rank):
    rows, block = spikes.shape
    full = lax.dot_general(
        spikes, factors, (((1,), (1,)), ((), ())), preferred_element_type=jnp.float32
    )
    kept = jnp.where(member_mask(rows, full.shape[1], trials, rank), full, 0.0)
    trial = lax.broadcasted_iota(jnp.int32, kept.shape, 0) % trials
    parts = [
        jnp.sum(jnp.where(trial == j, kept, 0.0), axis=0, keepdims=True) for j in range(trials)
    ]
    terms = three_terms(jnp.concatenate(parts, axis=0))
    pad = jnp.zeros((EXT - 3 * trials, block), jnp.float32)
    out_ref[:rows] = spikes
    out_ref[rows:] = jnp.concatenate([*terms, pad], axis=0).astype(jnp.bfloat16)


def pack_kernel(spikes_ref, factors_ref, out_ref, *, trials, rank):
    store_packed(out_ref, spikes_ref[...], factors_ref[...], trials, rank)


def pack(spikes, factors, trials, rank):
    rows, block = spikes.shape
    whole = pl.BlockSpec(memory_space=pltpu.VMEM)
    return pl.pallas_call(
        functools.partial(pack_kernel, trials=trials, rank=rank),
        out_shape=jax.ShapeDtypeStruct((rows + EXT, block), jnp.bfloat16),
        in_specs=[whole] * 2,
        out_specs=whole,
        compiler_params=pltpu.CompilerParams(vmem_limit_bytes=4 << 20),
        name="pack",
    )(spikes, factors)


def to_column(value, rows, trials):
    shape = (rows, value.shape[1])
    row = lax.broadcasted_iota(jnp.int32, shape, 0)
    kept = row // trials == lax.broadcasted_iota(jnp.int32, shape, 1)
    if value.shape[0] == 1:
        spread = jnp.broadcast_to(value, shape)
    else:
        spread = by_trial(value, rows)
    return jnp.sum(jnp.where(kept, spread, 0.0), axis=1, keepdims=True)


def update_kernel(*refs, step, trials, rank):
    keep_ref, came_ref, packed_ref, v_ref, a_ref, lanes_ref, ids_ref, count_ref = refs[:8]
    u_ref, f_ref, outs = refs[8], refs[9], refs[10:]
    rows, _ = v_ref.shape
    total = keep_ref[:rows] + came_ref[:rows].astype(jnp.float32)
    tail = came_ref[rows:].astype(jnp.float32)
    proj = keep_ref[rows : rows + trials]
    for term in range(3):
        proj = proj + tail[term * trials : (term + 1) * trials]
    mask = member_mask(rows, u_ref.shape[0], trials, rank)
    spread = jnp.where(mask, by_trial(proj, rows), 0.0).astype(jnp.bfloat16)
    low = jnp.dot(spread, u_ref[...], preferred_element_type=jnp.float32)
    current = by_trial(lanes_ref[4 + step * trials : 4 + (step + 1) * trials], rows)
    half_sign = to_column(0.5 - (ids_ref[...] & 1).astype(jnp.float32), rows, trials)
    count = to_column(count_ref[...].astype(jnp.float32), rows, trials)
    drive = total + half_sign * low + current
    decay_mem, decay_adapt = lanes_ref[0:1], lanes_ref[1:2]
    base, adapt = lanes_ref[2:3], lanes_ref[3:4]
    spikes = packed_ref[:rows].astype(jnp.float32)
    v, a = v_ref[...], a_ref[...]
    v_new = decay_mem * v + (1.0 - decay_mem) * drive - spikes * (base + adapt * a)
    active = count > float(step)
    v = jnp.where(active, v_new, v)
    outs[0][...] = v
    if len(outs) > 1:
        a_new = decay_adapt * a + (1.0 - decay_adapt) * spikes
        a = jnp.where(active, a_new, a)
        outs[1][...] = a
        fresh = jax.nn.sigmoid(3.0 * (v - base - adapt * a)).astype(jnp.bfloat16)
        store_packed(outs[2], fresh, f_ref[...], trials, rank)


def update(keep, came, packed, v, a, lanes, ids, count, u_rows, f_rows, step, trials, rank):
    state = jax.ShapeDtypeStruct(v.shape, jnp.float32)
    outs = [state]
    if step + 1 < STEPS:
        outs += [state, jax.ShapeDtypeStruct(packed.shape, packed.dtype)]
    whole = pl.BlockSpec(memory_space=pltpu.VMEM)
    return pl.pallas_call(
        functools.partial(update_kernel, step=step, trials=trials, rank=rank),
        out_shape=tuple(outs),
        in_specs=[whole] * 10,
        out_specs=(whole,) * len(outs),
        compiler_params=pltpu.CompilerParams(vmem_limit_bytes=6 << 20),
        name="update",
    )(keep, came, packed, v, a, lanes, ids, count, u_rows, f_rows)


def mix_kernel(at_ref, *refs, rows, trials, late):
    spikes, weights = refs[:4], refs[4:8]
    mine_ref, theirs_ref = refs[-2:]
    flip, shift, y = at_ref[0], at_ref[1], at_ref[2]
    tall, block = spikes[0].shape[1:]
    extra = None
    for q in range(4):
        tail = spikes[q][:2, rows:, :].astype(jnp.float32)
        tail = tail + spikes[q][2:, rows:, :].astype(jnp.float32)
        extra = tail if extra is None else extra + tail
    part = extra[:, :trials] + extra[:, trials : 2 * trials] + extra[:, 2 * trials : 3 * trials]

    def run(low):
        total = None
        for q in range(4):
            for high in range(2):
                first = ((shift >> 1) ^ high) * 2
                chunk = spikes[q][pl.ds(first, 2)]
                piece = jnp.dot(
                    chunk.reshape(2 * tall, block),
                    weights[2 * high + low][y ^ q],
                    preferred_element_type=jnp.float32,
                )
                total = piece if total is None else total + piece
        for s in range(2):
            for half, ref in enumerate((mine_ref, theirs_ref)):
                value = total[s * tall : (s + 1) * tall, half * block : (half + 1) * block]
                other = part[s]
                if late:
                    before = refs[8 + half]
                    value = value + before[s ^ flip]
                    other = other + before[s ^ flip, rows : rows + trials, :]
                ref[s ^ flip] = value
                ref[s ^ flip, rows : rows + trials, :] = other

    for low in range(2):
        pl.when(((shift & 1) ^ int(late)) == low)(functools.partial(run, low))


def mix(at, spikes, weights, rows, trials, before=()):
    blocks, tall, block = spikes[0].shape
    out = jax.ShapeDtypeStruct((2, tall, block), jnp.float32)
    whole = pl.BlockSpec(memory_space=pltpu.VMEM)
    inputs = len(spikes) * spikes[0].size + 2 * weights[0].size
    return pl.pallas_call(
        functools.partial(mix_kernel, rows=rows, trials=trials, late=len(before) > 0),
        out_shape=(out, out),
        in_specs=[pl.BlockSpec(memory_space=pltpu.SMEM)] + [whole] * (8 + len(before)),
        out_specs=(whole, whole),
        cost_estimate=pl.CostEstimate(
            flops=4 * blocks * tall * weights[0].size // 2,
            bytes_accessed=2 * inputs + 16 * tall * block,
            transcendentals=0,
        ),
        compiler_params=pltpu.CompilerParams(vmem_limit_bytes=12 << 20),
        name="mix_late" if before else "mix_early",
    )(at, *spikes, *weights, *before)


def fold_kernel(mine_ref, theirs_ref, keep_ref, give_ref, *, rows, trials):
    keep_ref[...] = mine_ref[0] + theirs_ref[0]
    give = mine_ref[1] + theirs_ref[1]
    terms = three_terms(give[rows : rows + trials])
    pad = jnp.zeros((EXT - 3 * trials, give.shape[1]), jnp.float32)
    give_ref[...] = jnp.concatenate([give[:rows], *terms, pad], axis=0).astype(jnp.bfloat16)


def fold(mine, theirs, rows, trials):
    shape = mine.shape[1:]
    whole = pl.BlockSpec(memory_space=pltpu.VMEM)
    return pl.pallas_call(
        functools.partial(fold_kernel, rows=rows, trials=trials),
        out_shape=(
            jax.ShapeDtypeStruct(shape, jnp.float32),
            jax.ShapeDtypeStruct(shape, jnp.bfloat16),
        ),
        in_specs=[whole, whole],
        out_specs=(whole, whole),
        compiler_params=pltpu.CompilerParams(vmem_limit_bytes=4 << 20),
        name="fold",
    )(mine, theirs)


def spread_weights(base_weight, at):
    outs, depth = base_weight.shape
    block = depth // 8
    split = base_weight.reshape(outs, 4, 2, block)
    one = at["c"] == 1
    keep = jnp.where(one, split[:, :, 1], split[:, :, 0]).transpose(1, 2, 0)
    give = jnp.where(one, split[:, :, 0], split[:, :, 1]).transpose(1, 2, 0)
    got = over_c(give)
    own = jnp.concatenate([keep, got], axis=2)
    chunks = [own]
    for k in (1, 2, 3):
        chunks.append(over_x(own, k))
    return chunks


def body(
    v_init,
    a_init,
    z_init,
    base_weight,
    factor_u,
    factor_v,
    in_weight,
    spikes_in,
    step_count,
    member_ids,
    decay_mem,
    decay_adapt,
    thr_base,
    thr_adapt,
):
    members, trials, block = v_init.shape
    rank = factor_u.shape[1]
    rows = members * trials
    at = {name: lax.axis_index(name) for name in AXES}
    u_rows = factor_u.reshape(members * rank, block)
    f_rows = factor_v.reshape(members * rank, block)
    ids = member_ids.reshape(1, members)
    count = step_count.T
    current = jnp.dot(
        spikes_in.reshape(STEPS * trials, -1).astype(jnp.bfloat16),
        in_weight,
        preferred_element_type=jnp.float32,
    )
    lanes = jnp.stack([decay_mem, decay_adapt, thr_base, thr_adapt])
    lanes = jnp.concatenate([lanes, current], axis=0)
    place = jnp.stack([at["a"] ^ at["zh"], at["b"] ^ at["x"], at["y"]])
    v, a = v_init.reshape(rows, block), a_init.reshape(rows, block)
    packed = pack(z_init.reshape(rows, block), f_rows, trials, rank)
    weights = spread_weights(base_weight, at)
    for step in range(STEPS):
        held = to_owner(packed)[None]
        other = over_a(held)
        held = jnp.concatenate([held, other], axis=0)
        other = over_b(held, 2)
        held = jnp.concatenate([held, other], axis=0)
        if step == 0:
            ready = (held, place, lanes, u_rows, v, a)
            held, place, lanes, u_rows, v, a = lax.optimization_barrier(ready)
        if step + 1 == STEPS:
            spikes_f = packed[:rows].astype(jnp.float32)
            a_new = decay_adapt * a + (1.0 - decay_adapt) * spikes_f
            a_new = a_new.reshape(a_init.shape)
            active = (step_count > step)[:, :, None]
            a_out = jnp.where(active, a_new, a.reshape(a_init.shape))
            held, a_out = lax.optimization_barrier((held, a_out))
        early = [held]
        late = [over_b(early[0], 1)]
        for pieces in (early, late):
            for k in (1, 2, 3):
                pieces.append(over_y(pieces[0], k))
        halves = mix(place, early, weights, rows, trials)
        mine, theirs = mix(place, late, weights, rows, trials, halves)
        theirs = over_c(theirs)
        keep, give = fold(mine, theirs, rows, trials)
        came = over_zh(give)
        v, *rest = update(
            keep, came, packed, v, a, lanes, ids, count, u_rows, f_rows, step, trials, rank
        )
        if rest:
            a, packed = rest
    return (v.reshape(v_init.shape), a_out)


def solution(mesh):
    fine = Mesh(mesh.devices.reshape(SIZES), AXES)
    in_specs = (
        P(POP, None, BLK),
        P(POP, None, BLK),
        P(POP, None, BLK),
        P(BLK, POP),
        P(POP, None, BLK),
        P(POP, None, BLK),
        P(None, BLK),
        P(),
        P(POP, None),
        P(POP),
        P(BLK),
        P(BLK),
        P(BLK),
        P(BLK),
    )
    out_specs = (P(POP, None, BLK), P(POP, None, BLK))
    return jax.shard_map(body, mesh=fine, in_specs=in_specs, out_specs=out_specs, check_vma=False)
```

```python
import functools

import jax
import jax.numpy as jnp
import numpy as np
from jax import lax
from jax.experimental import pallas as pl
from jax.experimental.pallas import tpu as pltpu
from jax.sharding import Mesh
from jax.sharding import PartitionSpec as P

STEPS = 2
AXES = ("zh", "x", "a", "b", "y", "c")
SIZES = (2, 4, 2, 4, 4, 2)
POP = ("zh", "x")
BLK = ("a", "b", "y", "c")
EXT = 8


def permute(value, dest):
    pairs = []
    for source in np.ndindex(*SIZES):
        there = dest(*source)
        pairs.append(
            (int(np.ravel_multi_index(source, SIZES)), int(np.ravel_multi_index(there, SIZES)))
        )
    return lax.ppermute(value, AXES, pairs)


def to_owner(value):
    return permute(value, lambda zh, x, a, b, y, c: (a, x, zh, b, y, c))


def over_a(value):
    return permute(value, lambda zh, x, a, b, y, c: (zh, x, 1 - a, b, y, c))


def over_b(value, k):
    return permute(value, lambda zh, x, a, b, y, c: (zh, x, a, b ^ k, y, c))


def over_y(value, k):
    return permute(value, lambda zh, x, a, b, y, c: (zh, x, a, b, y ^ k, c))


def over_c(value):
    return permute(value, lambda zh, x, a, b, y, c: (zh, x, a, b, y, 1 - c))


def over_x(value, k):
    return permute(value, lambda zh, x, a, b, y, c: (zh, x ^ k, a, b, y, c))


def over_zh(value):
    return permute(value, lambda zh, x, a, b, y, c: (1 - zh, x, a, b, y, c))


def member_mask(rows, cols, trials, rank):
    row = lax.broadcasted_iota(jnp.int32, (rows, cols), 0) // trials
    col = lax.broadcasted_iota(jnp.int32, (rows, cols), 1) // rank
    return row == col


def by_trial(values, rows):
    trials, block = values.shape
    trial = lax.broadcasted_iota(jnp.int32, (rows, block), 0) % trials
    out = jnp.broadcast_to(values[:1], (rows, block))
    for j in range(1, trials):
        out = jnp.where(trial == j, jnp.broadcast_to(values[j : j + 1], (rows, block)), out)
    return out


def three_terms(value):
    high = value.astype(jnp.bfloat16).astype(jnp.float32)
    rest = value - high
    middle = rest.astype(jnp.bfloat16).astype(jnp.float32)
    return [high, middle, rest - middle]


def store_packed(out_ref, spikes, factors, trials, rank):
    rows, block = spikes.shape
    full = lax.dot_general(
        spikes, factors, (((1,), (1,)), ((), ())), preferred_element_type=jnp.float32
    )
    kept = jnp.where(member_mask(rows, full.shape[1], trials, rank), full, 0.0)
    trial = lax.broadcasted_iota(jnp.int32, kept.shape, 0) % trials
    parts = [
        jnp.sum(jnp.where(trial == j, kept, 0.0), axis=0, keepdims=True) for j in range(trials)
    ]
    terms = three_terms(jnp.concatenate(parts, axis=0))
    pad = jnp.zeros((EXT - 3 * trials, block), jnp.float32)
    out_ref[:rows] = spikes
    out_ref[rows:] = jnp.concatenate([*terms, pad], axis=0).astype(jnp.bfloat16)


def pack_kernel(spikes_ref, factors_ref, out_ref, *, trials, rank):
    members, _, block = spikes_ref.shape
    spikes = spikes_ref[...].reshape(members * trials, block)
    store_packed(out_ref, spikes, factors_ref[...].reshape(members * rank, block), trials, rank)


def pack(spikes, factors):
    members, trials, block = spikes.shape
    rows, rank = members * trials, factors.shape[1]
    whole = pl.BlockSpec(memory_space=pltpu.VMEM)
    return pl.pallas_call(
        functools.partial(pack_kernel, trials=trials, rank=rank),
        out_shape=jax.ShapeDtypeStruct((rows + EXT, block), jnp.bfloat16),
        in_specs=[whole] * 2,
        out_specs=whole,
        compiler_params=pltpu.CompilerParams(vmem_limit_bytes=4 << 20),
        name="pack",
    )(spikes, factors)


def to_column(value, rows, trials):
    shape = (rows, value.shape[1])
    row = lax.broadcasted_iota(jnp.int32, shape, 0)
    kept = row // trials == lax.broadcasted_iota(jnp.int32, shape, 1)
    if value.shape[0] == 1:
        spread = jnp.broadcast_to(value, shape)
    else:
        spread = by_trial(value, rows)
    return jnp.sum(jnp.where(kept, spread, 0.0), axis=1, keepdims=True)


def update_kernel(*refs, step, trials, rank):
    keep_ref, came_ref, packed_ref, v_ref, a_ref, lanes_ref, ids_ref, count_ref = refs[:8]
    u_ref, f_ref, outs = refs[8], refs[9], refs[10:]
    members, _, block = u_ref.shape
    rows = members * trials
    total = keep_ref[:rows] + came_ref[:rows].astype(jnp.float32)
    tail = came_ref[rows:].astype(jnp.float32)
    proj = keep_ref[rows : rows + trials]
    for term in range(3):
        proj = proj + tail[term * trials : (term + 1) * trials]
    mask = member_mask(rows, members * rank, trials, rank)
    spread = jnp.where(mask, by_trial(proj, rows), 0.0).astype(jnp.bfloat16)
    u_rows = u_ref[...].reshape(members * rank, block)
    low = jnp.dot(spread, u_rows, preferred_element_type=jnp.float32)
    current = by_trial(lanes_ref[4 + step * trials : 4 + (step + 1) * trials], rows)
    half_sign = to_column(0.5 - (ids_ref[...] & 1).astype(jnp.float32), rows, trials)
    count = to_column(count_ref[...].astype(jnp.float32), rows, trials)
    drive = total + half_sign * low + current
    decay_mem, decay_adapt = lanes_ref[0:1], lanes_ref[1:2]
    base, adapt = lanes_ref[2:3], lanes_ref[3:4]
    spikes = packed_ref[:rows].astype(jnp.float32)
    v, a = v_ref[...].reshape(rows, block), a_ref[...].reshape(rows, block)
    v_new = decay_mem * v + (1.0 - decay_mem) * drive - spikes * (base + adapt * a)
    v = jnp.where(count > float(step), v_new, v)
    outs[0][...] = v.reshape(outs[0].shape)
    if step + 1 < STEPS:
        a_new = decay_adapt * a + (1.0 - decay_adapt) * spikes
        a = jnp.where(count > float(step), a_new, a)
        fresh = jax.nn.sigmoid(3.0 * (v - base - adapt * a)).astype(jnp.bfloat16)
        f_rows = f_ref[...].reshape(members * rank, block)
        store_packed(outs[1], fresh, f_rows, trials, rank)
        outs[2][...] = a
        if step + 2 == STEPS:
            a_new = decay_adapt * a + (1.0 - decay_adapt) * fresh.astype(jnp.float32)
            a = jnp.where(count > float(step + 1), a_new, a)
            outs[3][...] = a.reshape(outs[3].shape)


def update(keep, came, packed, v, a, lanes, ids, count, factor_u, factor_v, step):
    members, rank, block = factor_u.shape
    trials = count.shape[0]
    rows = jax.ShapeDtypeStruct((members * trials, block), jnp.float32)
    final = jax.ShapeDtypeStruct((members, trials, block), jnp.float32)
    if step + 1 < STEPS:
        outs = [rows, jax.ShapeDtypeStruct(packed.shape, packed.dtype), rows]
        outs += [final] if step + 2 == STEPS else []
    else:
        outs = [final]
    whole = pl.BlockSpec(memory_space=pltpu.VMEM)
    return pl.pallas_call(
        functools.partial(update_kernel, step=step, trials=trials, rank=rank),
        out_shape=tuple(outs),
        in_specs=[whole] * 10,
        out_specs=(whole,) * len(outs),
        compiler_params=pltpu.CompilerParams(vmem_limit_bytes=6 << 20),
        name="update",
    )(keep, came, packed, v, a, lanes, ids, count, factor_u, factor_v)


def mix_kernel(at_ref, *refs, pieces, rows, trials, late):
    spikes, weights = refs[: 4 * pieces], refs[4 * pieces : 4 * pieces + 4]
    mine_ref, theirs_ref = refs[-2:]
    before = refs[-4:-2]
    flip, shift, y = at_ref[0], at_ref[1], at_ref[2]
    tall, block = spikes[0].shape[1:]
    depth = spikes[0].shape[0] // 2
    extra = None
    for ref in spikes:
        for pair in range(depth):
            tail = ref[2 * pair : 2 * pair + 2, rows:, :].astype(jnp.float32)
            extra = tail if extra is None else extra + tail
    part = extra[:, :trials] + extra[:, trials : 2 * trials] + extra[:, 2 * trials : 3 * trials]

    def run(there):
        total = None
        for q in range(4):
            for high in range(2):
                ref = spikes[q + 4 * high] if pieces == 2 else spikes[q]
                chunk = ref[...] if pieces == 2 else ref[2 * high : 2 * high + 2]
                piece = jnp.dot(
                    chunk.reshape(2 * tall, block),
                    weights[there ^ (2 * high + int(late))][y ^ q],
                    preferred_element_type=jnp.float32,
                )
                total = piece if total is None else total + piece
        for s in range(2):
            for half, ref in enumerate((mine_ref, theirs_ref)):
                value = total[s * tall : (s + 1) * tall, half * block : (half + 1) * block]
                other = part[s]
                if late:
                    value = value + before[half][s ^ flip]
                    other = other + before[half][s ^ flip, rows : rows + trials, :]
                ref[s ^ flip] = value
                ref[s ^ flip, rows : rows + trials, :] = other

    for there in range(4):
        pl.when(shift == there)(functools.partial(run, there))


def mix(at, spikes, weights, rows, trials, before=()):
    _, tall, block = spikes[0].shape
    out = jax.ShapeDtypeStruct((2, tall, block), jnp.float32)
    whole = pl.BlockSpec(memory_space=pltpu.VMEM)
    inputs = len(spikes) * spikes[0].size + 2 * weights[0].size
    return pl.pallas_call(
        functools.partial(
            mix_kernel, pieces=len(spikes) // 4, rows=rows, trials=trials, late=len(before) > 0
        ),
        out_shape=(out, out),
        in_specs=[pl.BlockSpec(memory_space=pltpu.SMEM)]
        + [whole] * (len(spikes) + 4 + len(before)),
        out_specs=(whole, whole),
        cost_estimate=pl.CostEstimate(
            flops=16 * tall * weights[0].size // 2,
            bytes_accessed=2 * inputs + 16 * tall * block,
            transcendentals=0,
        ),
        compiler_params=pltpu.CompilerParams(vmem_limit_bytes=12 << 20),
        name="mix_late" if before else "mix_early",
    )(at, *spikes, *weights, *before)


def fold_kernel(mine_ref, theirs_ref, keep_ref, give_ref, *, rows, trials):
    keep_ref[...] = mine_ref[0] + theirs_ref[0]
    give = mine_ref[1] + theirs_ref[1]
    terms = three_terms(give[rows : rows + trials])
    pad = jnp.zeros((EXT - 3 * trials, give.shape[1]), jnp.float32)
    give_ref[...] = jnp.concatenate([give[:rows], *terms, pad], axis=0).astype(jnp.bfloat16)


def fold(mine, theirs, rows, trials):
    shape = mine.shape[1:]
    whole = pl.BlockSpec(memory_space=pltpu.VMEM)
    return pl.pallas_call(
        functools.partial(fold_kernel, rows=rows, trials=trials),
        out_shape=(
            jax.ShapeDtypeStruct(shape, jnp.float32),
            jax.ShapeDtypeStruct(shape, jnp.bfloat16),
        ),
        in_specs=[whole, whole],
        out_specs=(whole, whole),
        compiler_params=pltpu.CompilerParams(vmem_limit_bytes=4 << 20),
        name="fold",
    )(mine, theirs)


def spread_weights(base_weight, at):
    outs, depth = base_weight.shape
    block = depth // 8
    split = base_weight.reshape(outs, 4, 2, block)
    one = at["c"] == 1
    keep = jnp.where(one, split[:, :, 1], split[:, :, 0]).transpose(1, 2, 0)
    give = jnp.where(one, split[:, :, 0], split[:, :, 1]).transpose(1, 2, 0)
    got = over_c(give)
    own = jnp.concatenate([keep, got], axis=2)
    chunks = [own]
    for k in (1, 2, 3):
        chunks.append(over_x(own, k))
    return chunks


def body(
    v_init,
    a_init,
    z_init,
    base_weight,
    factor_u,
    factor_v,
    in_weight,
    spikes_in,
    step_count,
    member_ids,
    decay_mem,
    decay_adapt,
    thr_base,
    thr_adapt,
):
    members, trials, _ = v_init.shape
    rows = members * trials
    at = {name: lax.axis_index(name) for name in AXES}
    ids = member_ids.reshape(1, members)
    count = step_count.T
    current = jnp.dot(
        spikes_in.reshape(STEPS * trials, -1).astype(jnp.bfloat16),
        in_weight,
        preferred_element_type=jnp.float32,
    )
    lanes = jnp.stack([decay_mem, decay_adapt, thr_base, thr_adapt])
    lanes = jnp.concatenate([lanes, current], axis=0)
    place = jnp.stack([at["a"] ^ at["zh"], at["b"] ^ at["x"], at["y"]])
    v, a = v_init, a_init
    packed = pack(z_init, factor_v)
    weights = spread_weights(base_weight, at)
    for step in range(STEPS):
        held = to_owner(packed)[None]
        other = over_a(held)
        first = [jnp.concatenate([held, other], axis=0)]
        second = [over_b(first[0], 2)]
        held = jnp.concatenate([first[0], second[0]], axis=0)
        if step == 0:
            held, place, lanes = lax.optimization_barrier((held, place, lanes))
        last = [over_b(held, 1)]
        for pieces in (first, second, last):
            for k in (1, 2, 3):
                pieces.append(over_y(pieces[0], k))
        halves = mix(place, first + second, weights, rows, trials)
        mine, theirs = mix(place, last, weights, rows, trials, halves)
        theirs = over_c(theirs)
        keep, give = fold(mine, theirs, rows, trials)
        came = over_zh(give)
        v, *rest = update(
            keep, came, packed, v, a, lanes, ids, count, factor_u, factor_v, step
        )
        if rest:
            packed, a, *ends = rest
            a_out = ends[0] if ends else None
    return (v, a_out)


def solution(mesh):
    fine = Mesh(mesh.devices.reshape(SIZES), AXES)
    in_specs = (
        P(POP, None, BLK),
        P(POP, None, BLK),
        P(POP, None, BLK),
        P(BLK, POP),
        P(POP, None, BLK),
        P(POP, None, BLK),
        P(None, BLK),
        P(),
        P(POP, None),
        P(POP),
        P(BLK),
        P(BLK),
        P(BLK),
        P(BLK),
    )
    out_specs = (P(POP, None, BLK), P(POP, None, BLK))
    return jax.shard_map(body, mesh=fine, in_specs=in_specs, out_specs=out_specs, check_vma=False)
```

```python
import functools

import jax
import jax.numpy as jnp
import numpy as np
from jax import lax
from jax.experimental import pallas as pl
from jax.experimental.pallas import tpu as pltpu
from jax.sharding import Mesh
from jax.sharding import PartitionSpec as P

STEPS = 2
AXES = ("zh", "x", "a", "b", "y", "c")
SIZES = (2, 4, 2, 4, 4, 2)
POP = ("zh", "x")
BLK = ("a", "b", "y", "c")
EXT = 8


def permute(value, dest):
    pairs = []
    for source in np.ndindex(*SIZES):
        there = dest(*source)
        pairs.append(
            (int(np.ravel_multi_index(source, SIZES)), int(np.ravel_multi_index(there, SIZES)))
        )
    return lax.ppermute(value, AXES, pairs)


def to_owner(value):
    return permute(value, lambda zh, x, a, b, y, c: (a, x, zh, b, y, c))


def over_a(value):
    return permute(value, lambda zh, x, a, b, y, c: (zh, x, 1 - a, b, y, c))


def over_b(value, k):
    return permute(value, lambda zh, x, a, b, y, c: (zh, x, a, b ^ k, y, c))


def over_y(value, k):
    return permute(value, lambda zh, x, a, b, y, c: (zh, x, a, b, y ^ k, c))


def over_c(value):
    return permute(value, lambda zh, x, a, b, y, c: (zh, x, a, b, y, 1 - c))


def over_x(value, k):
    return permute(value, lambda zh, x, a, b, y, c: (zh, x ^ k, a, b, y, c))


def over_zh(value):
    return permute(value, lambda zh, x, a, b, y, c: (1 - zh, x, a, b, y, c))


def member_mask(rows, cols, trials, rank):
    row = lax.broadcasted_iota(jnp.int32, (rows, cols), 0) // trials
    col = lax.broadcasted_iota(jnp.int32, (rows, cols), 1) // rank
    return row == col


def by_trial(values, rows):
    trials, block = values.shape
    trial = lax.broadcasted_iota(jnp.int32, (rows, block), 0) % trials
    out = jnp.broadcast_to(values[:1], (rows, block))
    for j in range(1, trials):
        out = jnp.where(trial == j, jnp.broadcast_to(values[j : j + 1], (rows, block)), out)
    return out


def three_terms(value):
    high = value.astype(jnp.bfloat16).astype(jnp.float32)
    rest = value - high
    middle = rest.astype(jnp.bfloat16).astype(jnp.float32)
    return [high, middle, rest - middle]


def store_packed(out_ref, spikes, factors, trials, rank):
    rows, block = spikes.shape
    full = lax.dot_general(
        spikes, factors, (((1,), (1,)), ((), ())), preferred_element_type=jnp.float32
    )
    kept = jnp.where(member_mask(rows, full.shape[1], trials, rank), full, 0.0)
    trial = lax.broadcasted_iota(jnp.int32, kept.shape, 0) % trials
    parts = [
        jnp.sum(jnp.where(trial == j, kept, 0.0), axis=0, keepdims=True) for j in range(trials)
    ]
    terms = three_terms(jnp.concatenate(parts, axis=0))
    pad = jnp.zeros((EXT - 3 * trials, block), jnp.float32)
    out_ref[:rows] = spikes
    out_ref[rows:] = jnp.concatenate([*terms, pad], axis=0).astype(jnp.bfloat16)


def pack_kernel(spikes_ref, factors_ref, out_ref, *, trials, rank):
    members, _, block = spikes_ref.shape
    spikes = spikes_ref[...].reshape(members * trials, block)
    store_packed(out_ref, spikes, factors_ref[...].reshape(members * rank, block), trials, rank)


def pack(spikes, factors):
    members, trials, block = spikes.shape
    rows, rank = members * trials, factors.shape[1]
    whole = pl.BlockSpec(memory_space=pltpu.VMEM)
    return pl.pallas_call(
        functools.partial(pack_kernel, trials=trials, rank=rank),
        out_shape=jax.ShapeDtypeStruct((rows + EXT, block), jnp.bfloat16),
        in_specs=[whole] * 2,
        out_specs=whole,
        compiler_params=pltpu.CompilerParams(vmem_limit_bytes=4 << 20),
        name="pack",
    )(spikes, factors)


def to_column(value, rows, trials):
    shape = (rows, value.shape[1])
    row = lax.broadcasted_iota(jnp.int32, shape, 0)
    kept = row // trials == lax.broadcasted_iota(jnp.int32, shape, 1)
    if value.shape[0] == 1:
        spread = jnp.broadcast_to(value, shape)
    else:
        spread = by_trial(value, rows)
    return jnp.sum(jnp.where(kept, spread, 0.0), axis=1, keepdims=True)


def update_kernel(*refs, step, trials, rank):
    keep_ref, came_ref, packed_ref, v_ref, a_ref, lanes_ref, ids_ref, count_ref = refs[:8]
    u_ref, f_ref, outs = refs[8], refs[9], refs[10:]
    members, _, block = u_ref.shape
    rows = members * trials
    total = keep_ref[:rows] + came_ref[:rows].astype(jnp.float32)
    tail = came_ref[rows:].astype(jnp.float32)
    proj = keep_ref[rows : rows + trials]
    for term in range(3):
        proj = proj + tail[term * trials : (term + 1) * trials]
    mask = member_mask(rows, members * rank, trials, rank)
    spread = jnp.where(mask, by_trial(proj, rows), 0.0).astype(jnp.bfloat16)
    u_rows = u_ref[...].reshape(members * rank, block)
    low = jnp.dot(spread, u_rows, preferred_element_type=jnp.float32)
    current = by_trial(lanes_ref[4 + step * trials : 4 + (step + 1) * trials], rows)
    half_sign = to_column(0.5 - (ids_ref[...] & 1).astype(jnp.float32), rows, trials)
    count = to_column(count_ref[...].astype(jnp.float32), rows, trials)
    drive = total + half_sign * low + current
    decay_mem, decay_adapt = lanes_ref[0:1], lanes_ref[1:2]
    base, adapt = lanes_ref[2:3], lanes_ref[3:4]
    spikes = packed_ref[:rows].astype(jnp.float32)
    v, a = v_ref[...].reshape(rows, block), a_ref[...].reshape(rows, block)
    v_new = decay_mem * v + (1.0 - decay_mem) * drive - spikes * (base + adapt * a)
    v = jnp.where(count > float(step), v_new, v)
    outs[0][...] = v.reshape(outs[0].shape)
    if step + 1 < STEPS:
        a_new = decay_adapt * a + (1.0 - decay_adapt) * spikes
        a = jnp.where(count > float(step), a_new, a)
        fresh = jax.nn.sigmoid(3.0 * (v - base - adapt * a)).astype(jnp.bfloat16)
        f_rows = f_ref[...].reshape(members * rank, block)
        store_packed(outs[1], fresh, f_rows, trials, rank)
        outs[2][...] = a
        if step + 2 == STEPS:
            a_new = decay_adapt * a + (1.0 - decay_adapt) * fresh.astype(jnp.float32)
            a = jnp.where(count > float(step + 1), a_new, a)
            outs[3][...] = a.reshape(outs[3].shape)


def update(keep, came, packed, v, a, lanes, ids, count, factor_u, factor_v, step):
    members, rank, block = factor_u.shape
    trials = count.shape[0]
    rows = jax.ShapeDtypeStruct((members * trials, block), jnp.float32)
    final = jax.ShapeDtypeStruct((members, trials, block), jnp.float32)
    if step + 1 < STEPS:
        outs = [rows, jax.ShapeDtypeStruct(packed.shape, packed.dtype), rows]
        outs += [final] if step + 2 == STEPS else []
    else:
        outs = [final]
    whole = pl.BlockSpec(memory_space=pltpu.VMEM)
    return pl.pallas_call(
        functools.partial(update_kernel, step=step, trials=trials, rank=rank),
        out_shape=tuple(outs),
        in_specs=[whole] * 10,
        out_specs=(whole,) * len(outs),
        compiler_params=pltpu.CompilerParams(vmem_limit_bytes=6 << 20),
        name="update",
    )(keep, came, packed, v, a, lanes, ids, count, factor_u, factor_v)


def mix_kernel(at_ref, *refs, pieces, rows, trials, late):
    spikes, weights = refs[: 4 * pieces], refs[4 * pieces : 4 * pieces + 4]
    mine_ref, theirs_ref = refs[-2:]
    before = refs[-4:-2]
    flip, shift, y = at_ref[0], at_ref[1], at_ref[2]
    tall, block = spikes[0].shape[1:]
    depth = spikes[0].shape[0] // 2
    extra = None
    for ref in spikes:
        for pair in range(depth):
            tail = ref[2 * pair : 2 * pair + 2, rows:, :].astype(jnp.float32)
            extra = tail if extra is None else extra + tail
    part = extra[:, :trials] + extra[:, trials : 2 * trials] + extra[:, 2 * trials : 3 * trials]

    def run(there):
        total = None
        for q in range(4):
            for high in range(2):
                ref = spikes[q + 4 * high] if pieces == 2 else spikes[q]
                chunk = ref[...] if pieces == 2 else ref[2 * high : 2 * high + 2]
                piece = jnp.dot(
                    chunk.reshape(2 * tall, block),
                    weights[there ^ (2 * high + int(late))][y ^ q],
                    preferred_element_type=jnp.float32,
                )
                total = piece if total is None else total + piece
        for s in range(2):
            for half, ref in enumerate((mine_ref, theirs_ref)):
                value = total[s * tall : (s + 1) * tall, half * block : (half + 1) * block]
                other = part[s]
                if late:
                    value = value + before[half][s ^ flip]
                    other = other + before[half][s ^ flip, rows : rows + trials, :]
                ref[s ^ flip] = value
                ref[s ^ flip, rows : rows + trials, :] = other

    for there in range(4):
        pl.when(shift == there)(functools.partial(run, there))


def mix(at, spikes, weights, rows, trials, before=()):
    _, tall, block = spikes[0].shape
    out = jax.ShapeDtypeStruct((2, tall, block), jnp.float32)
    whole = pl.BlockSpec(memory_space=pltpu.VMEM)
    inputs = len(spikes) * spikes[0].size + 2 * weights[0].size
    return pl.pallas_call(
        functools.partial(
            mix_kernel, pieces=len(spikes) // 4, rows=rows, trials=trials, late=len(before) > 0
        ),
        out_shape=(out, out),
        in_specs=[pl.BlockSpec(memory_space=pltpu.SMEM)]
        + [whole] * (len(spikes) + 4 + len(before)),
        out_specs=(whole, whole),
        cost_estimate=pl.CostEstimate(
            flops=16 * tall * weights[0].size // 2,
            bytes_accessed=2 * inputs + 16 * tall * block,
            transcendentals=0,
        ),
        compiler_params=pltpu.CompilerParams(vmem_limit_bytes=12 << 20),
        name="mix_late" if before else "mix_early",
    )(at, *spikes, *weights, *before)


def fold_kernel(mine_ref, theirs_ref, keep_ref, give_ref, *, rows, trials):
    keep_ref[...] = mine_ref[0] + theirs_ref[0]
    give = mine_ref[1] + theirs_ref[1]
    terms = three_terms(give[rows : rows + trials])
    pad = jnp.zeros((EXT - 3 * trials, give.shape[1]), jnp.float32)
    give_ref[...] = jnp.concatenate([give[:rows], *terms, pad], axis=0).astype(jnp.bfloat16)


def fold(mine, theirs, rows, trials):
    shape = mine.shape[1:]
    whole = pl.BlockSpec(memory_space=pltpu.VMEM)
    return pl.pallas_call(
        functools.partial(fold_kernel, rows=rows, trials=trials),
        out_shape=(
            jax.ShapeDtypeStruct(shape, jnp.float32),
            jax.ShapeDtypeStruct(shape, jnp.bfloat16),
        ),
        in_specs=[whole, whole],
        out_specs=(whole, whole),
        compiler_params=pltpu.CompilerParams(vmem_limit_bytes=4 << 20),
        name="fold",
    )(mine, theirs)


def spread_weights(base_weight, at):
    outs, depth = base_weight.shape
    block = depth // 8
    split = base_weight.reshape(outs, 4, 2, block)
    one = at["c"] == 1
    keep = jnp.where(one, split[:, :, 1], split[:, :, 0]).transpose(1, 2, 0)
    give = jnp.where(one, split[:, :, 0], split[:, :, 1]).transpose(1, 2, 0)
    got = over_c(give)
    own = jnp.concatenate([keep, got], axis=2)
    chunks = [own]
    for k in (1, 2, 3):
        chunks.append(over_x(own, k))
    return chunks


def body(
    v_init,
    a_init,
    z_init,
    base_weight,
    factor_u,
    factor_v,
    in_weight,
    spikes_in,
    step_count,
    member_ids,
    decay_mem,
    decay_adapt,
    thr_base,
    thr_adapt,
):
    members, trials, _ = v_init.shape
    rows = members * trials
    at = {name: lax.axis_index(name) for name in AXES}
    ids = member_ids.reshape(1, members)
    count = step_count.T
    current = jnp.dot(
        spikes_in.reshape(STEPS * trials, -1).astype(jnp.bfloat16),
        in_weight,
        preferred_element_type=jnp.float32,
    )
    lanes = jnp.stack([decay_mem, decay_adapt, thr_base, thr_adapt])
    lanes = jnp.concatenate([lanes, current], axis=0)
    place = jnp.stack([at["a"] ^ at["zh"], at["b"] ^ at["x"], at["y"]])
    v, a = v_init, a_init
    packed = pack(z_init, factor_v)
    weights = spread_weights(base_weight, at)
    for step in range(STEPS):
        held = to_owner(packed)[None]
        other = over_a(held)
        first = [jnp.concatenate([held, other], axis=0)]
        second = [over_b(first[0], 2)]
        held = jnp.concatenate([first[0], second[0]], axis=0)
        if step == 0:
            held, place, lanes = lax.optimization_barrier((held, place, lanes))
        last = [over_b(held, 1)]
        for pieces, near, far in ((first, 1, 3), (second, 3, 1)):
            came = {}
            for k in (near, far):
                came[k] = over_y(pieces[0], k)
            came[2] = over_y(came[near], far)
            pieces += [came[k] for k in (1, 2, 3)]
        for k in (1, 2, 3):
            last.append(over_y(last[0], k))
        halves = mix(place, first + second, weights, rows, trials)
        mine, theirs = mix(place, last, weights, rows, trials, halves)
        theirs = over_c(theirs)
        keep, give = fold(mine, theirs, rows, trials)
        came = over_zh(give)
        v, *rest = update(
            keep, came, packed, v, a, lanes, ids, count, factor_u, factor_v, step
        )
        if rest:
            packed, a, *ends = rest
            a_out = ends[0] if ends else None
    return (v, a_out)


def solution(mesh):
    fine = Mesh(mesh.devices.reshape(SIZES), AXES)
    in_specs = (
        P(POP, None, BLK),
        P(POP, None, BLK),
        P(POP, None, BLK),
        P(BLK, POP),
        P(POP, None, BLK),
        P(POP, None, BLK),
        P(None, BLK),
        P(),
        P(POP, None),
        P(POP),
        P(BLK),
        P(BLK),
        P(BLK),
        P(BLK),
    )
    out_specs = (P(POP, None, BLK), P(POP, None, BLK))
    return jax.shard_map(body, mesh=fine, in_specs=in_specs, out_specs=out_specs, check_vma=False)
```

```python
import functools

import jax
import jax.numpy as jnp
import numpy as np
from jax import lax
from jax.experimental import pallas as pl
from jax.experimental.pallas import tpu as pltpu
from jax.sharding import Mesh
from jax.sharding import PartitionSpec as P

STEPS = 2
AXES = ("zh", "x", "a", "b", "y", "c")
SIZES = (2, 4, 2, 4, 4, 2)
POP = ("zh", "x")
BLK = ("a", "b", "y", "c")
EXT = 8


def permute(value, dest):
    pairs = []
    for source in np.ndindex(*SIZES):
        there = dest(*source)
        pairs.append(
            (int(np.ravel_multi_index(source, SIZES)), int(np.ravel_multi_index(there, SIZES)))
        )
    return lax.ppermute(value, AXES, pairs)


def some(value, pick, dest):
    pairs = []
    for source in np.ndindex(*SIZES):
        if pick(*source):
            there = np.ravel_multi_index(dest(*source), SIZES)
            pairs.append((int(np.ravel_multi_index(source, SIZES)), int(there)))
    return lax.ppermute(value, AXES, pairs)


def to_owner(value):
    there = lambda zh, x, a, b, y, c: (a, x, zh, b, y, c)
    return some(value, lambda zh, x, a, b, y, c: zh != a, there)


def outward(value, middle):
    there = lambda zh, x, a, b, y, c: (zh, x, 1 - a, b, y, c)
    return some(value, lambda zh, x, a, b, y, c: (zh != a) == middle, there)


def over_b(value, k):
    return permute(value, lambda zh, x, a, b, y, c: (zh, x, a, b ^ k, y, c))


def over_y(value, k):
    return permute(value, lambda zh, x, a, b, y, c: (zh, x, a, b, y ^ k, c))


def over_c(value):
    return permute(value, lambda zh, x, a, b, y, c: (zh, x, a, b, y, 1 - c))


def over_x(value, k):
    return permute(value, lambda zh, x, a, b, y, c: (zh, x ^ k, a, b, y, c))


def over_zh(value):
    return permute(value, lambda zh, x, a, b, y, c: (1 - zh, x, a, b, y, c))


def member_mask(rows, cols, trials, rank):
    row = lax.broadcasted_iota(jnp.int32, (rows, cols), 0) // trials
    col = lax.broadcasted_iota(jnp.int32, (rows, cols), 1) // rank
    return row == col


def by_trial(values, rows):
    trials, block = values.shape
    trial = lax.broadcasted_iota(jnp.int32, (rows, block), 0) % trials
    out = jnp.broadcast_to(values[:1], (rows, block))
    for j in range(1, trials):
        out = jnp.where(trial == j, jnp.broadcast_to(values[j : j + 1], (rows, block)), out)
    return out


def three_terms(value):
    high = value.astype(jnp.bfloat16).astype(jnp.float32)
    rest = value - high
    middle = rest.astype(jnp.bfloat16).astype(jnp.float32)
    return [high, middle, rest - middle]


def store_packed(out_ref, spikes, factors, trials, rank):
    rows, block = spikes.shape
    full = lax.dot_general(
        spikes, factors, (((1,), (1,)), ((), ())), preferred_element_type=jnp.float32
    )
    kept = jnp.where(member_mask(rows, full.shape[1], trials, rank), full, 0.0)
    trial = lax.broadcasted_iota(jnp.int32, kept.shape, 0) % trials
    parts = [
        jnp.sum(jnp.where(trial == j, kept, 0.0), axis=0, keepdims=True) for j in range(trials)
    ]
    terms = three_terms(jnp.concatenate(parts, axis=0))
    pad = jnp.zeros((EXT - 3 * trials, block), jnp.float32)
    out_ref[:rows] = spikes
    out_ref[rows:] = jnp.concatenate([*terms, pad], axis=0).astype(jnp.bfloat16)


def pack_kernel(spikes_ref, factors_ref, out_ref, *, trials, rank):
    members, _, block = spikes_ref.shape
    spikes = spikes_ref[...].reshape(members * trials, block)
    store_packed(out_ref, spikes, factors_ref[...].reshape(members * rank, block), trials, rank)


def pack(spikes, factors):
    members, trials, block = spikes.shape
    rows, rank = members * trials, factors.shape[1]
    whole = pl.BlockSpec(memory_space=pltpu.VMEM)
    return pl.pallas_call(
        functools.partial(pack_kernel, trials=trials, rank=rank),
        out_shape=jax.ShapeDtypeStruct((rows + EXT, block), jnp.bfloat16),
        in_specs=[whole] * 2,
        out_specs=whole,
        compiler_params=pltpu.CompilerParams(vmem_limit_bytes=4 << 20),
        name="pack",
    )(spikes, factors)


def to_column(value, rows, trials):
    shape = (rows, value.shape[1])
    row = lax.broadcasted_iota(jnp.int32, shape, 0)
    kept = row // trials == lax.broadcasted_iota(jnp.int32, shape, 1)
    if value.shape[0] == 1:
        spread = jnp.broadcast_to(value, shape)
    else:
        spread = by_trial(value, rows)
    return jnp.sum(jnp.where(kept, spread, 0.0), axis=1, keepdims=True)


def update_kernel(*refs, step, trials, rank):
    mine_ref, theirs_ref, came_ref, packed_ref, v_ref, a_ref = refs[:6]
    lanes_ref, ids_ref, count_ref, u_ref, f_ref = refs[6:11]
    outs = refs[11:]
    members, _, block = u_ref.shape
    rows = members * trials
    total = mine_ref[:rows] + theirs_ref[:rows] + came_ref[:rows].astype(jnp.float32)
    tail = came_ref[rows:].astype(jnp.float32)
    proj = mine_ref[rows : rows + trials] + theirs_ref[rows : rows + trials]
    for term in range(3):
        proj = proj + tail[term * trials : (term + 1) * trials]
    mask = member_mask(rows, members * rank, trials, rank)
    spread = jnp.where(mask, by_trial(proj, rows), 0.0).astype(jnp.bfloat16)
    u_rows = u_ref[...].reshape(members * rank, block)
    low = jnp.dot(spread, u_rows, preferred_element_type=jnp.float32)
    current = by_trial(lanes_ref[4 + step * trials : 4 + (step + 1) * trials], rows)
    half_sign = to_column(0.5 - (ids_ref[...] & 1).astype(jnp.float32), rows, trials)
    count = to_column(count_ref[...].astype(jnp.float32), rows, trials)
    drive = total + half_sign * low + current
    decay_mem, decay_adapt = lanes_ref[0:1], lanes_ref[1:2]
    base, adapt = lanes_ref[2:3], lanes_ref[3:4]
    spikes = packed_ref[:rows].astype(jnp.float32)
    v, a = v_ref[...].reshape(rows, block), a_ref[...].reshape(rows, block)
    v_new = decay_mem * v + (1.0 - decay_mem) * drive - spikes * (base + adapt * a)
    v = jnp.where(count > float(step), v_new, v)
    outs[0][...] = v.reshape(outs[0].shape)
    if step + 1 < STEPS:
        a_new = decay_adapt * a + (1.0 - decay_adapt) * spikes
        a = jnp.where(count > float(step), a_new, a)
        fresh = jax.nn.sigmoid(3.0 * (v - base - adapt * a)).astype(jnp.bfloat16)
        f_rows = f_ref[...].reshape(members * rank, block)
        store_packed(outs[1], fresh, f_rows, trials, rank)
        outs[2][...] = a
        if step + 2 == STEPS:
            a_new = decay_adapt * a + (1.0 - decay_adapt) * fresh.astype(jnp.float32)
            a = jnp.where(count > float(step + 1), a_new, a)
            outs[3][...] = a.reshape(outs[3].shape)


def update(mine, theirs, came, packed, v, a, lanes, ids, count, factor_u, factor_v, step):
    members, rank, block = factor_u.shape
    trials = count.shape[0]
    rows = jax.ShapeDtypeStruct((members * trials, block), jnp.float32)
    final = jax.ShapeDtypeStruct((members, trials, block), jnp.float32)
    if step + 1 < STEPS:
        outs = [rows, jax.ShapeDtypeStruct(packed.shape, packed.dtype), rows]
        outs += [final] if step + 2 == STEPS else []
    else:
        outs = [final]
    whole = pl.BlockSpec(memory_space=pltpu.VMEM)
    return pl.pallas_call(
        functools.partial(update_kernel, step=step, trials=trials, rank=rank),
        out_shape=tuple(outs),
        in_specs=[whole] * 11,
        out_specs=(whole,) * len(outs),
        compiler_params=pltpu.CompilerParams(vmem_limit_bytes=6 << 20),
        name="update",
    )(mine, theirs, came, packed, v, a, lanes, ids, count, factor_u, factor_v)


def mix_kernel(at_ref, *refs, pieces, rows, trials):
    spikes, weights = refs[: 4 * pieces], refs[4 * pieces : 4 * pieces + 4]
    mine_ref, theirs_ref = refs[-2:]
    shift, y = at_ref[0], at_ref[1]
    block = spikes[0].shape[2]
    part = None
    for ref in spikes:
        for k in range(ref.shape[0]):
            tail = ref[k, rows:, :].astype(jnp.float32)
            part = tail if part is None else part + tail
    part = part[:trials] + part[trials : 2 * trials] + part[2 * trials : 3 * trials]

    def run(odd):
        total = None
        for q in range(4):
            for k in range(4):
                low, high = (k & 1) ^ odd, (shift >> 1) ^ (k >> 1)
                if pieces == 2:
                    chunk = spikes[q + 4 * low][high]
                else:
                    chunk = spikes[q][2 * low + high]
                piece = jnp.dot(
                    chunk, weights[k][y ^ q], preferred_element_type=jnp.float32
                )
                total = piece if total is None else total + piece
        for half, ref in enumerate((mine_ref, theirs_ref)):
            ref[...] = total[:, half * block : (half + 1) * block]
            ref[rows : rows + trials, :] = part

    for odd in range(2):
        pl.when((shift & 1) == odd)(functools.partial(run, odd))


def mix(at, spikes, weights, rows, trials):
    tall, block = spikes[0].shape[1:]
    out = jax.ShapeDtypeStruct((tall, block), jnp.float32)
    whole = pl.BlockSpec(memory_space=pltpu.VMEM)
    inputs = len(spikes) * spikes[0].size + 4 * weights[0].size
    return pl.pallas_call(
        functools.partial(mix_kernel, pieces=len(spikes) // 4, rows=rows, trials=trials),
        out_shape=(out, out),
        in_specs=[pl.BlockSpec(memory_space=pltpu.SMEM)] + [whole] * (len(spikes) + 4),
        out_specs=(whole, whole),
        cost_estimate=pl.CostEstimate(
            flops=8 * tall * weights[0].size,
            bytes_accessed=2 * inputs + 8 * tall * block,
            transcendentals=0,
        ),
        compiler_params=pltpu.CompilerParams(vmem_limit_bytes=12 << 20),
    )(at, *spikes, *weights)


def fold_kernel(mine_ref, theirs_ref, give_ref, *, rows, trials):
    give = mine_ref[...] + theirs_ref[...]
    terms = three_terms(give[rows : rows + trials])
    pad = jnp.zeros((EXT - 3 * trials, give.shape[1]), jnp.float32)
    give_ref[...] = jnp.concatenate([give[:rows], *terms, pad], axis=0).astype(jnp.bfloat16)


def fold(mine, theirs, rows, trials):
    whole = pl.BlockSpec(memory_space=pltpu.VMEM)
    return pl.pallas_call(
        functools.partial(fold_kernel, rows=rows, trials=trials),
        out_shape=jax.ShapeDtypeStruct(mine.shape, jnp.bfloat16),
        in_specs=[whole, whole],
        out_specs=whole,
        compiler_params=pltpu.CompilerParams(vmem_limit_bytes=4 << 20),
        name="fold",
    )(mine, theirs)


def spread_weights(base_weight, at):
    outs, depth = base_weight.shape
    block = depth // 8
    split = base_weight.reshape(outs, 4, 2, block)
    one = at["c"] == 1
    keep = jnp.where(one, split[:, :, 1], split[:, :, 0]).transpose(1, 2, 0)
    give = jnp.where(one, split[:, :, 0], split[:, :, 1]).transpose(1, 2, 0)
    got = over_c(give)
    own = jnp.concatenate([keep, got], axis=2)
    chunks = [own]
    for k in (1, 2, 3):
        chunks.append(over_x(own, k))
    return chunks


def body(
    v_init,
    a_init,
    z_init,
    base_weight,
    factor_u,
    factor_v,
    in_weight,
    spikes_in,
    step_count,
    member_ids,
    decay_mem,
    decay_adapt,
    thr_base,
    thr_adapt,
):
    members, trials, _ = v_init.shape
    rows = members * trials
    at = {name: lax.axis_index(name) for name in AXES}
    ids = member_ids.reshape(1, members)
    count = step_count.T
    current = jnp.dot(
        spikes_in.reshape(STEPS * trials, -1).astype(jnp.bfloat16),
        in_weight,
        preferred_element_type=jnp.float32,
    )
    lanes = jnp.stack([decay_mem, decay_adapt, thr_base, thr_adapt])
    lanes = jnp.concatenate([lanes, current], axis=0)
    place = jnp.stack([at["b"] ^ at["x"], at["y"]])
    outer = at["zh"] == at["a"]
    v, a = v_init, a_init
    packed = pack(z_init, factor_v)
    weights = spread_weights(base_weight, at)
    for step in range(STEPS):
        crossed = to_owner(packed)
        stayed = outward(packed, False)
        relayed = outward(crossed, True)
        keep = jnp.where(outer, packed, stayed)[None]
        give = jnp.where(outer, relayed, crossed)[None]
        keep = jnp.concatenate([keep, over_b(keep, 2)], axis=0)
        keep = [jnp.concatenate([keep, over_b(keep, 1)], axis=0)]
        half = [jnp.concatenate([give, over_b(give, 2)], axis=0)]
        if step == 0:
            half[0], place, lanes = lax.optimization_barrier((half[0], place, lanes))
        last = [over_b(half[0], 1)]
        for pieces, near, far in ((keep, 1, 3), (half, 3, 1)):
            came = {}
            for k in (near, far):
                came[k] = over_y(pieces[0], k)
            came[2] = over_y(came[near], far)
            pieces += [came[k] for k in (1, 2, 3)]
        for k in (1, 2, 3):
            last.append(over_y(last[0], k))
        mine, theirs = mix(place, half + last, weights, rows, trials)
        theirs = over_c(theirs)
        give = fold(mine, theirs, rows, trials)
        came = over_zh(give)
        mine, theirs = mix(place, keep, weights, rows, trials)
        theirs = over_c(theirs)
        v, *rest = update(
            mine, theirs, came, packed, v, a, lanes, ids, count, factor_u, factor_v, step
        )
        if rest:
            packed, a, *ends = rest
            a_out = ends[0] if ends else None
    return (v, a_out)


def solution(mesh):
    fine = Mesh(mesh.devices.reshape(SIZES), AXES)
    in_specs = (
        P(POP, None, BLK),
        P(POP, None, BLK),
        P(POP, None, BLK),
        P(BLK, POP),
        P(POP, None, BLK),
        P(POP, None, BLK),
        P(None, BLK),
        P(),
        P(POP, None),
        P(POP),
        P(BLK),
        P(BLK),
        P(BLK),
        P(BLK),
    )
    out_specs = (P(POP, None, BLK), P(POP, None, BLK))
    return jax.shard_map(body, mesh=fine, in_specs=in_specs, out_specs=out_specs, check_vma=False)
```

```python
import functools

import jax
import jax.numpy as jnp
import numpy as np
from jax import lax
from jax.experimental import pallas as pl
from jax.experimental.pallas import tpu as pltpu
from jax.sharding import Mesh
from jax.sharding import PartitionSpec as P

STEPS = 2
AXES = ("zh", "x", "a", "b", "y", "c")
SIZES = (2, 4, 2, 4, 4, 2)
POP = ("zh", "x")
BLK = ("a", "b", "y", "c")
EXT = 8


def permute(value, dest):
    pairs = []
    for source in np.ndindex(*SIZES):
        there = dest(*source)
        pairs.append(
            (int(np.ravel_multi_index(source, SIZES)), int(np.ravel_multi_index(there, SIZES)))
        )
    return lax.ppermute(value, AXES, pairs)


def some(value, pick, dest):
    pairs = []
    for source in np.ndindex(*SIZES):
        if pick(*source):
            there = np.ravel_multi_index(dest(*source), SIZES)
            pairs.append((int(np.ravel_multi_index(source, SIZES)), int(there)))
    return lax.ppermute(value, AXES, pairs)


def to_owner(value):
    there = lambda zh, x, a, b, y, c: (a, x, zh, b, y, c)
    return some(value, lambda zh, x, a, b, y, c: zh != a, there)


def outward(value, middle):
    there = lambda zh, x, a, b, y, c: (zh, x, 1 - a, b, y, c)
    return some(value, lambda zh, x, a, b, y, c: (zh != a) == middle, there)


def over_b(value, k):
    return permute(value, lambda zh, x, a, b, y, c: (zh, x, a, b ^ k, y, c))


def over_y(value, k):
    return permute(value, lambda zh, x, a, b, y, c: (zh, x, a, b, y ^ k, c))


def over_c(value):
    return permute(value, lambda zh, x, a, b, y, c: (zh, x, a, b, y, 1 - c))


def over_x(value, k):
    return permute(value, lambda zh, x, a, b, y, c: (zh, x ^ k, a, b, y, c))


def over_zh(value):
    return permute(value, lambda zh, x, a, b, y, c: (1 - zh, x, a, b, y, c))


def member_mask(rows, cols, trials, rank):
    row = lax.broadcasted_iota(jnp.int32, (rows, cols), 0) // trials
    col = lax.broadcasted_iota(jnp.int32, (rows, cols), 1) // rank
    return row == col


def by_trial(values, rows):
    trials, block = values.shape
    trial = lax.broadcasted_iota(jnp.int32, (rows, block), 0) % trials
    out = jnp.broadcast_to(values[:1], (rows, block))
    for j in range(1, trials):
        out = jnp.where(trial == j, jnp.broadcast_to(values[j : j + 1], (rows, block)), out)
    return out


def three_terms(value):
    high = value.astype(jnp.bfloat16).astype(jnp.float32)
    rest = value - high
    middle = rest.astype(jnp.bfloat16).astype(jnp.float32)
    return [high, middle, rest - middle]


def store_packed(out_ref, spikes, factors, trials, rank):
    rows, block = spikes.shape
    full = lax.dot_general(
        spikes, factors, (((1,), (1,)), ((), ())), preferred_element_type=jnp.float32
    )
    kept = jnp.where(member_mask(rows, full.shape[1], trials, rank), full, 0.0)
    trial = lax.broadcasted_iota(jnp.int32, kept.shape, 0) % trials
    parts = [
        jnp.sum(jnp.where(trial == j, kept, 0.0), axis=0, keepdims=True) for j in range(trials)
    ]
    terms = three_terms(jnp.concatenate(parts, axis=0))
    pad = jnp.zeros((EXT - 3 * trials, block), jnp.float32)
    out_ref[:rows] = spikes
    out_ref[rows:] = jnp.concatenate([*terms, pad], axis=0).astype(jnp.bfloat16)


def pack_kernel(spikes_ref, factors_ref, out_ref, *, trials, rank):
    members, _, block = spikes_ref.shape
    spikes = spikes_ref[...].reshape(members * trials, block)
    store_packed(out_ref, spikes, factors_ref[...].reshape(members * rank, block), trials, rank)


def pack(spikes, factors):
    members, trials, block = spikes.shape
    rows, rank = members * trials, factors.shape[1]
    whole = pl.BlockSpec(memory_space=pltpu.VMEM)
    return pl.pallas_call(
        functools.partial(pack_kernel, trials=trials, rank=rank),
        out_shape=jax.ShapeDtypeStruct((rows + EXT, block), jnp.bfloat16),
        in_specs=[whole] * 2,
        out_specs=whole,
        compiler_params=pltpu.CompilerParams(vmem_limit_bytes=4 << 20),
        name="pack",
    )(spikes, factors)


def to_column(value, rows, trials):
    shape = (rows, value.shape[1])
    row = lax.broadcasted_iota(jnp.int32, shape, 0)
    kept = row // trials == lax.broadcasted_iota(jnp.int32, shape, 1)
    if value.shape[0] == 1:
        spread = jnp.broadcast_to(value, shape)
    else:
        spread = by_trial(value, rows)
    return jnp.sum(jnp.where(kept, spread, 0.0), axis=1, keepdims=True)


def update_kernel(*refs, step, trials, rank):
    mine_ref, theirs_ref, came_ref, packed_ref, v_ref, a_ref = refs[:6]
    lanes_ref, ids_ref, count_ref, u_ref, f_ref = refs[6:11]
    outs = refs[11:]
    members, _, block = u_ref.shape
    rows = members * trials
    total = mine_ref[:rows] + theirs_ref[:rows] + came_ref[:rows].astype(jnp.float32)
    tail = came_ref[rows:].astype(jnp.float32)
    proj = mine_ref[rows : rows + trials] + theirs_ref[rows : rows + trials]
    for term in range(3):
        proj = proj + tail[term * trials : (term + 1) * trials]
    mask = member_mask(rows, members * rank, trials, rank)
    spread = jnp.where(mask, by_trial(proj, rows), 0.0).astype(jnp.bfloat16)
    u_rows = u_ref[...].reshape(members * rank, block)
    low = jnp.dot(spread, u_rows, preferred_element_type=jnp.float32)
    current = by_trial(lanes_ref[4 + step * trials : 4 + (step + 1) * trials], rows)
    half_sign = to_column(0.5 - (ids_ref[...] & 1).astype(jnp.float32), rows, trials)
    count = to_column(count_ref[...].astype(jnp.float32), rows, trials)
    drive = total + half_sign * low + current
    decay_mem, decay_adapt = lanes_ref[0:1], lanes_ref[1:2]
    base, adapt = lanes_ref[2:3], lanes_ref[3:4]
    spikes = packed_ref[:rows].astype(jnp.float32)
    v, a = v_ref[...].reshape(rows, block), a_ref[...].reshape(rows, block)
    v_new = decay_mem * v + (1.0 - decay_mem) * drive - spikes * (base + adapt * a)
    v = jnp.where(count > float(step), v_new, v)
    outs[0][...] = v.reshape(outs[0].shape)
    if step + 1 < STEPS:
        a_new = decay_adapt * a + (1.0 - decay_adapt) * spikes
        a = jnp.where(count > float(step), a_new, a)
        fresh = jax.nn.sigmoid(3.0 * (v - base - adapt * a)).astype(jnp.bfloat16)
        f_rows = f_ref[...].reshape(members * rank, block)
        store_packed(outs[1], fresh, f_rows, trials, rank)
        outs[2][...] = a
        if step + 2 == STEPS:
            a_new = decay_adapt * a + (1.0 - decay_adapt) * fresh.astype(jnp.float32)
            a = jnp.where(count > float(step + 1), a_new, a)
            outs[3][...] = a.reshape(outs[3].shape)


def update(mine, theirs, came, packed, v, a, lanes, ids, count, factor_u, factor_v, step):
    members, rank, block = factor_u.shape
    trials = count.shape[0]
    rows = jax.ShapeDtypeStruct((members * trials, block), jnp.float32)
    final = jax.ShapeDtypeStruct((members, trials, block), jnp.float32)
    if step + 1 < STEPS:
        outs = [rows, jax.ShapeDtypeStruct(packed.shape, packed.dtype), rows]
        outs += [final] if step + 2 == STEPS else []
    else:
        outs = [final]
    whole = pl.BlockSpec(memory_space=pltpu.VMEM)
    return pl.pallas_call(
        functools.partial(update_kernel, step=step, trials=trials, rank=rank),
        out_shape=tuple(outs),
        in_specs=[whole] * 11,
        out_specs=(whole,) * len(outs),
        compiler_params=pltpu.CompilerParams(vmem_limit_bytes=6 << 20),
        name="update",
    )(mine, theirs, came, packed, v, a, lanes, ids, count, factor_u, factor_v)


def mix_kernel(at_ref, *refs, pieces, rows, trials):
    spikes, weights = refs[: 4 * pieces], refs[4 * pieces : 4 * pieces + 4]
    mine_ref, theirs_ref = refs[-2:]
    shift, y = at_ref[0], at_ref[1]
    block = spikes[0].shape[2]
    part = None
    for ref in spikes:
        for k in range(ref.shape[0]):
            tail = ref[k, rows:, :].astype(jnp.float32)
            part = tail if part is None else part + tail
    part = part[:trials] + part[trials : 2 * trials] + part[2 * trials : 3 * trials]

    def run(odd):
        total = None
        for q in range(4):
            for k in range(4):
                low, high = (k & 1) ^ odd, (shift >> 1) ^ (k >> 1)
                if pieces == 2:
                    chunk = spikes[q + 4 * low][high]
                else:
                    chunk = spikes[q][2 * low + high]
                piece = jnp.dot(
                    chunk, weights[k][y ^ q], preferred_element_type=jnp.float32
                )
                total = piece if total is None else total + piece
        for half, ref in enumerate((mine_ref, theirs_ref)):
            ref[...] = total[:, half * block : (half + 1) * block]
            ref[rows : rows + trials, :] = part

    for odd in range(2):
        pl.when((shift & 1) == odd)(functools.partial(run, odd))


def mix(at, spikes, weights, rows, trials):
    tall, block = spikes[0].shape[1:]
    out = jax.ShapeDtypeStruct((tall, block), jnp.float32)
    whole = pl.BlockSpec(memory_space=pltpu.VMEM)
    inputs = len(spikes) * spikes[0].size + 4 * weights[0].size
    return pl.pallas_call(
        functools.partial(mix_kernel, pieces=len(spikes) // 4, rows=rows, trials=trials),
        out_shape=(out, out),
        in_specs=[pl.BlockSpec(memory_space=pltpu.SMEM)] + [whole] * (len(spikes) + 4),
        out_specs=(whole, whole),
        cost_estimate=pl.CostEstimate(
            flops=8 * tall * weights[0].size,
            bytes_accessed=2 * inputs + 8 * tall * block,
            transcendentals=0,
        ),
        compiler_params=pltpu.CompilerParams(vmem_limit_bytes=12 << 20),
    )(at, *spikes, *weights)


def fold_kernel(mine_ref, theirs_ref, give_ref, *, rows, trials):
    give = mine_ref[...] + theirs_ref[...]
    terms = three_terms(give[rows : rows + trials])
    pad = jnp.zeros((EXT - 3 * trials, give.shape[1]), jnp.float32)
    give_ref[...] = jnp.concatenate([give[:rows], *terms, pad], axis=0).astype(jnp.bfloat16)


def fold(mine, theirs, rows, trials):
    whole = pl.BlockSpec(memory_space=pltpu.VMEM)
    return pl.pallas_call(
        functools.partial(fold_kernel, rows=rows, trials=trials),
        out_shape=jax.ShapeDtypeStruct(mine.shape, jnp.bfloat16),
        in_specs=[whole, whole],
        out_specs=whole,
        compiler_params=pltpu.CompilerParams(vmem_limit_bytes=4 << 20),
        name="fold",
    )(mine, theirs)


def spread_weights(base_weight, at):
    outs, depth = base_weight.shape
    block = depth // 8
    split = base_weight.reshape(outs, 4, 2, block)
    one = at["c"] == 1
    keep = jnp.where(one, split[:, :, 1], split[:, :, 0]).transpose(1, 2, 0)
    give = jnp.where(one, split[:, :, 0], split[:, :, 1]).transpose(1, 2, 0)
    got = over_c(give)
    own = jnp.concatenate([keep, got], axis=2)
    chunks = [own]
    for k in (1, 2, 3):
        chunks.append(over_x(own, k))
    return chunks


def body(
    v_init,
    a_init,
    z_init,
    base_weight,
    factor_u,
    factor_v,
    in_weight,
    spikes_in,
    step_count,
    member_ids,
    decay_mem,
    decay_adapt,
    thr_base,
    thr_adapt,
):
    members, trials, _ = v_init.shape
    rows = members * trials
    at = {name: lax.axis_index(name) for name in AXES}
    ids = member_ids.reshape(1, members)
    count = step_count.T
    current = jnp.dot(
        spikes_in.reshape(STEPS * trials, -1).astype(jnp.bfloat16),
        in_weight,
        preferred_element_type=jnp.float32,
    )
    lanes = jnp.stack([decay_mem, decay_adapt, thr_base, thr_adapt])
    lanes = jnp.concatenate([lanes, current], axis=0)
    place = jnp.stack([at["b"] ^ at["x"], at["y"]])
    outer = at["zh"] == at["a"]
    v, a = v_init, a_init
    packed = pack(z_init, factor_v)
    weights = spread_weights(base_weight, at)
    for step in range(STEPS):
        crossed = to_owner(packed)
        stayed = outward(packed, False)
        relayed = outward(crossed, True)
        keep = jnp.where(outer, packed, stayed)[None]
        give = jnp.where(outer, relayed, crossed)[None]
        keep = jnp.concatenate([keep, over_b(keep, 2)], axis=0)
        keep = [jnp.concatenate([keep, over_b(keep, 1)], axis=0)]
        half = [jnp.concatenate([give, over_b(give, 2)], axis=0)]
        if step == 0:
            half[0], place, lanes = lax.optimization_barrier((half[0], place, lanes))
        last = [over_b(half[0], 1)]
        came = {}
        for k in (3, 1):
            came[k] = over_y(half[0], k)
        came[2] = over_y(came[3], 1)
        half += [came[k] for k in (1, 2, 3)]
        for pieces in (last, keep):
            for k in (1, 2, 3):
                pieces.append(over_y(pieces[0], k))
        mine, theirs = mix(place, half + last, weights, rows, trials)
        theirs = over_c(theirs)
        give = fold(mine, theirs, rows, trials)
        came = over_zh(give)
        mine, theirs = mix(place, keep, weights, rows, trials)
        theirs = over_c(theirs)
        v, *rest = update(
            mine, theirs, came, packed, v, a, lanes, ids, count, factor_u, factor_v, step
        )
        if rest:
            packed, a, *ends = rest
            a_out = ends[0] if ends else None
    return (v, a_out)


def solution(mesh):
    fine = Mesh(mesh.devices.reshape(SIZES), AXES)
    in_specs = (
        P(POP, None, BLK),
        P(POP, None, BLK),
        P(POP, None, BLK),
        P(BLK, POP),
        P(POP, None, BLK),
        P(POP, None, BLK),
        P(None, BLK),
        P(),
        P(POP, None),
        P(POP),
        P(BLK),
        P(BLK),
        P(BLK),
        P(BLK),
    )
    out_specs = (P(POP, None, BLK), P(POP, None, BLK))
    return jax.shard_map(body, mesh=fine, in_specs=in_specs, out_specs=out_specs, check_vma=False)
```

```python
import functools

import jax
import jax.numpy as jnp
import numpy as np
from jax import lax
from jax.experimental import pallas as pl
from jax.experimental.pallas import tpu as pltpu
from jax.sharding import Mesh
from jax.sharding import PartitionSpec as P

STEPS = 2
AXES = ("zh", "x", "a", "b", "y", "c")
SIZES = (2, 4, 2, 4, 4, 2)
POP = ("zh", "x")
BLK = ("a", "b", "y", "c")
EXT = 8


def permute(value, dest):
    pairs = []
    for source in np.ndindex(*SIZES):
        there = dest(*source)
        pairs.append(
            (int(np.ravel_multi_index(source, SIZES)), int(np.ravel_multi_index(there, SIZES)))
        )
    return lax.ppermute(value, AXES, pairs)


def to_owner(value):
    return permute(value, lambda zh, x, a, b, y, c: (a, x, zh, b, y, c))


def over_a(value):
    return permute(value, lambda zh, x, a, b, y, c: (zh, x, 1 - a, b, y, c))


def over_b(value, k):
    return permute(value, lambda zh, x, a, b, y, c: (zh, x, a, b ^ k, y, c))


def over_y(value, k):
    return permute(value, lambda zh, x, a, b, y, c: (zh, x, a, b, y ^ k, c))


def over_c(value):
    return permute(value, lambda zh, x, a, b, y, c: (zh, x, a, b, y, 1 - c))


def over_x(value, k):
    return permute(value, lambda zh, x, a, b, y, c: (zh, x ^ k, a, b, y, c))


def over_zh(value):
    return permute(value, lambda zh, x, a, b, y, c: (1 - zh, x, a, b, y, c))


def member_mask(rows, cols, trials, rank):
    row = lax.broadcasted_iota(jnp.int32, (rows, cols), 0) // trials
    col = lax.broadcasted_iota(jnp.int32, (rows, cols), 1) // rank
    return row == col


def by_trial(values, rows):
    trials, block = values.shape
    trial = lax.broadcasted_iota(jnp.int32, (rows, block), 0) % trials
    out = jnp.broadcast_to(values[:1], (rows, block))
    for j in range(1, trials):
        out = jnp.where(trial == j, jnp.broadcast_to(values[j : j + 1], (rows, block)), out)
    return out


def three_terms(value):
    high = value.astype(jnp.bfloat16).astype(jnp.float32)
    rest = value - high
    middle = rest.astype(jnp.bfloat16).astype(jnp.float32)
    return [high, middle, rest - middle]


def store_packed(out_ref, spikes, factors, trials, rank):
    rows, block = spikes.shape
    full = lax.dot_general(
        spikes, factors, (((1,), (1,)), ((), ())), preferred_element_type=jnp.float32
    )
    kept = jnp.where(member_mask(rows, full.shape[1], trials, rank), full, 0.0)
    trial = lax.broadcasted_iota(jnp.int32, kept.shape, 0) % trials
    parts = [
        jnp.sum(jnp.where(trial == j, kept, 0.0), axis=0, keepdims=True) for j in range(trials)
    ]
    terms = three_terms(jnp.concatenate(parts, axis=0))
    pad = jnp.zeros((EXT - 3 * trials, block), jnp.float32)
    out_ref[:rows] = spikes
    out_ref[rows:] = jnp.concatenate([*terms, pad], axis=0).astype(jnp.bfloat16)


def pack_kernel(spikes_ref, factors_ref, out_ref, *, trials, rank):
    members, _, block = spikes_ref.shape
    spikes = spikes_ref[...].reshape(members * trials, block)
    store_packed(out_ref, spikes, factors_ref[...].reshape(members * rank, block), trials, rank)


def pack(spikes, factors):
    members, trials, block = spikes.shape
    rows, rank = members * trials, factors.shape[1]
    whole = pl.BlockSpec(memory_space=pltpu.VMEM)
    return pl.pallas_call(
        functools.partial(pack_kernel, trials=trials, rank=rank),
        out_shape=jax.ShapeDtypeStruct((rows + EXT, block), jnp.bfloat16),
        in_specs=[whole] * 2,
        out_specs=whole,
        compiler_params=pltpu.CompilerParams(vmem_limit_bytes=4 << 20),
        name="pack",
    )(spikes, factors)


def to_column(value, rows, trials):
    shape = (rows, value.shape[1])
    row = lax.broadcasted_iota(jnp.int32, shape, 0)
    kept = row // trials == lax.broadcasted_iota(jnp.int32, shape, 1)
    if value.shape[0] == 1:
        spread = jnp.broadcast_to(value, shape)
    else:
        spread = by_trial(value, rows)
    return jnp.sum(jnp.where(kept, spread, 0.0), axis=1, keepdims=True)


def update_kernel(*refs, step, trials, rank):
    keep_ref, came_ref, packed_ref, v_ref, a_ref, lanes_ref, ids_ref, count_ref = refs[:8]
    u_ref, f_ref, outs = refs[8], refs[9], refs[10:]
    members, _, block = u_ref.shape
    rows = members * trials
    total = keep_ref[:rows] + came_ref[:rows].astype(jnp.float32)
    tail = came_ref[rows:].astype(jnp.float32)
    proj = keep_ref[rows : rows + trials]
    for term in range(3):
        proj = proj + tail[term * trials : (term + 1) * trials]
    mask = member_mask(rows, members * rank, trials, rank)
    spread = jnp.where(mask, by_trial(proj, rows), 0.0).astype(jnp.bfloat16)
    u_rows = u_ref[...].reshape(members * rank, block)
    low = jnp.dot(spread, u_rows, preferred_element_type=jnp.float32)
    current = by_trial(lanes_ref[4 + step * trials : 4 + (step + 1) * trials], rows)
    half_sign = to_column(0.5 - (ids_ref[...] & 1).astype(jnp.float32), rows, trials)
    count = to_column(count_ref[...].astype(jnp.float32), rows, trials)
    drive = total + half_sign * low + current
    decay_mem, decay_adapt = lanes_ref[0:1], lanes_ref[1:2]
    base, adapt = lanes_ref[2:3], lanes_ref[3:4]
    spikes = packed_ref[:rows].astype(jnp.float32)
    v, a = v_ref[...].reshape(rows, block), a_ref[...].reshape(rows, block)
    v_new = decay_mem * v + (1.0 - decay_mem) * drive - spikes * (base + adapt * a)
    v = jnp.where(count > float(step), v_new, v)
    outs[0][...] = v.reshape(outs[0].shape)
    if step + 1 < STEPS:
        a_new = decay_adapt * a + (1.0 - decay_adapt) * spikes
        a = jnp.where(count > float(step), a_new, a)
        fresh = jax.nn.sigmoid(3.0 * (v - base - adapt * a)).astype(jnp.bfloat16)
        f_rows = f_ref[...].reshape(members * rank, block)
        store_packed(outs[1], fresh, f_rows, trials, rank)
        outs[2][...] = a
        if step + 2 == STEPS:
            a_new = decay_adapt * a + (1.0 - decay_adapt) * fresh.astype(jnp.float32)
            a = jnp.where(count > float(step + 1), a_new, a)
            outs[3][...] = a.reshape(outs[3].shape)


def update(keep, came, packed, v, a, lanes, ids, count, factor_u, factor_v, step):
    members, rank, block = factor_u.shape
    trials = count.shape[0]
    rows = jax.ShapeDtypeStruct((members * trials, block), jnp.float32)
    final = jax.ShapeDtypeStruct((members, trials, block), jnp.float32)
    if step + 1 < STEPS:
        outs = [rows, jax.ShapeDtypeStruct(packed.shape, packed.dtype), rows]
        outs += [final] if step + 2 == STEPS else []
    else:
        outs = [final]
    whole = pl.BlockSpec(memory_space=pltpu.VMEM)
    return pl.pallas_call(
        functools.partial(update_kernel, step=step, trials=trials, rank=rank),
        out_shape=tuple(outs),
        in_specs=[whole] * 10,
        out_specs=(whole,) * len(outs),
        compiler_params=pltpu.CompilerParams(vmem_limit_bytes=6 << 20),
        name="update",
    )(keep, came, packed, v, a, lanes, ids, count, factor_u, factor_v)


def mix_kernel(at_ref, *refs, pairs, rows, trials, late):
    spikes, weights = refs[:8], refs[8:12]
    mine_ref, theirs_ref = refs[-2:]
    before = refs[-4:-2]
    flip, shift, y = at_ref[0], at_ref[1], at_ref[2]
    tall, block = spikes[0].shape[1:]
    extra = None
    for ref in spikes:
        tail = ref[:, rows:, :].astype(jnp.float32)
        extra = tail if extra is None else extra + tail
    part = extra[:, :trials] + extra[:, trials : 2 * trials] + extra[:, 2 * trials : 3 * trials]

    def run(there):
        total = None
        for q in range(4):
            for i, pair in enumerate(pairs):
                piece = jnp.dot(
                    spikes[q + 4 * i][...].reshape(2 * tall, block),
                    weights[there ^ pair][y ^ q],
                    preferred_element_type=jnp.float32,
                )
                total = piece if total is None else total + piece
        for s in range(2):
            for half, ref in enumerate((mine_ref, theirs_ref)):
                value = total[s * tall : (s + 1) * tall, half * block : (half + 1) * block]
                other = part[s]
                if late:
                    value = value + before[half][s ^ flip]
                    other = other + before[half][s ^ flip, rows : rows + trials, :]
                ref[s ^ flip] = value
                ref[s ^ flip, rows : rows + trials, :] = other

    for there in range(4):
        pl.when(shift == there)(functools.partial(run, there))


def mix(at, spikes, weights, rows, trials, pairs, before=()):
    _, tall, block = spikes[0].shape
    out = jax.ShapeDtypeStruct((2, tall, block), jnp.float32)
    whole = pl.BlockSpec(memory_space=pltpu.VMEM)
    inputs = len(spikes) * spikes[0].size + 2 * weights[0].size
    return pl.pallas_call(
        functools.partial(
            mix_kernel, pairs=pairs, rows=rows, trials=trials, late=len(before) > 0
        ),
        out_shape=(out, out),
        in_specs=[pl.BlockSpec(memory_space=pltpu.SMEM)]
        + [whole] * (len(spikes) + 4 + len(before)),
        out_specs=(whole, whole),
        cost_estimate=pl.CostEstimate(
            flops=16 * tall * weights[0].size // 2,
            bytes_accessed=2 * inputs + 16 * tall * block,
            transcendentals=0,
        ),
        compiler_params=pltpu.CompilerParams(vmem_limit_bytes=12 << 20),
        name="mix_late" if before else "mix_early",
    )(at, *spikes, *weights, *before)


def fold_kernel(mine_ref, theirs_ref, keep_ref, give_ref, *, rows, trials):
    keep_ref[...] = mine_ref[0] + theirs_ref[0]
    give = mine_ref[1] + theirs_ref[1]
    terms = three_terms(give[rows : rows + trials])
    pad = jnp.zeros((EXT - 3 * trials, give.shape[1]), jnp.float32)
    give_ref[...] = jnp.concatenate([give[:rows], *terms, pad], axis=0).astype(jnp.bfloat16)


def fold(mine, theirs, rows, trials):
    shape = mine.shape[1:]
    whole = pl.BlockSpec(memory_space=pltpu.VMEM)
    return pl.pallas_call(
        functools.partial(fold_kernel, rows=rows, trials=trials),
        out_shape=(
            jax.ShapeDtypeStruct(shape, jnp.float32),
            jax.ShapeDtypeStruct(shape, jnp.bfloat16),
        ),
        in_specs=[whole, whole],
        out_specs=(whole, whole),
        compiler_params=pltpu.CompilerParams(vmem_limit_bytes=4 << 20),
        name="fold",
    )(mine, theirs)


def spread_weights(base_weight, at):
    outs, depth = base_weight.shape
    block = depth // 8
    split = base_weight.reshape(outs, 4, 2, block)
    one = at["c"] == 1
    keep = jnp.where(one, split[:, :, 1], split[:, :, 0]).transpose(1, 2, 0)
    give = jnp.where(one, split[:, :, 0], split[:, :, 1]).transpose(1, 2, 0)
    got = over_c(give)
    own = jnp.concatenate([keep, got], axis=2)
    chunks = [own]
    for k in (1, 2, 3):
        chunks.append(over_x(own, k))
    return chunks


def body(
    v_init,
    a_init,
    z_init,
    base_weight,
    factor_u,
    factor_v,
    in_weight,
    spikes_in,
    step_count,
    member_ids,
    decay_mem,
    decay_adapt,
    thr_base,
    thr_adapt,
):
    members, trials, _ = v_init.shape
    rows = members * trials
    at = {name: lax.axis_index(name) for name in AXES}
    ids = member_ids.reshape(1, members)
    count = step_count.T
    current = jnp.dot(
        spikes_in.reshape(STEPS * trials, -1).astype(jnp.bfloat16),
        in_weight,
        preferred_element_type=jnp.float32,
    )
    lanes = jnp.stack([decay_mem, decay_adapt, thr_base, thr_adapt])
    lanes = jnp.concatenate([lanes, current], axis=0)
    place = jnp.stack([at["a"] ^ at["zh"], at["b"] ^ at["x"], at["y"]])
    v, a = v_init, a_init
    packed = pack(z_init, factor_v)
    weights = spread_weights(base_weight, at)
    for step in range(STEPS):
        held = to_owner(packed)[None]
        other = over_a(held)
        pairs = {0: jnp.concatenate([held, other], axis=0)}
        pairs[2] = over_b(pairs[0], 2)
        pairs[1] = over_b(pairs[0], 1)
        if step == 0:
            pairs[2], place, lanes = lax.optimization_barrier((pairs[2], place, lanes))
        pairs[3] = over_b(pairs[2], 1)
        spread = {}
        for j in range(4):
            near, far = (3, 1) if j >= 2 else (1, 3)
            came = {0: pairs[j]}
            for k in (near, far):
                came[k] = over_y(pairs[j], k)
            came[2] = over_y(came[near], far)
            spread[j] = [came[k] for k in range(4)]
        early, late = spread[0] + spread[1], spread[2] + spread[3]
        halves = mix(place, early, weights, rows, trials, (0, 1))
        mine, theirs = mix(place, late, weights, rows, trials, (2, 3), halves)
        theirs = over_c(theirs)
        keep, give = fold(mine, theirs, rows, trials)
        came = over_zh(give)
        v, *rest = update(
            keep, came, packed, v, a, lanes, ids, count, factor_u, factor_v, step
        )
        if rest:
            packed, a, *ends = rest
            a_out = ends[0] if ends else None
    return (v, a_out)


def solution(mesh):
    fine = Mesh(mesh.devices.reshape(SIZES), AXES)
    in_specs = (
        P(POP, None, BLK),
        P(POP, None, BLK),
        P(POP, None, BLK),
        P(BLK, POP),
        P(POP, None, BLK),
        P(POP, None, BLK),
        P(None, BLK),
        P(),
        P(POP, None),
        P(POP),
        P(BLK),
        P(BLK),
        P(BLK),
        P(BLK),
    )
    out_specs = (P(POP, None, BLK), P(POP, None, BLK))
    return jax.shard_map(body, mesh=fine, in_specs=in_specs, out_specs=out_specs, check_vma=False)
```

```python
import functools

import jax
import jax.numpy as jnp
import numpy as np
from jax import lax
from jax.experimental import pallas as pl
from jax.experimental.pallas import tpu as pltpu
from jax.sharding import Mesh
from jax.sharding import PartitionSpec as P

STEPS = 2
AXES = ("zh", "x", "a", "b", "y", "c")
SIZES = (2, 4, 2, 4, 4, 2)
POP = ("zh", "x")
BLK = ("a", "b", "y", "c")
EXT = 8


def permute(value, dest):
    pairs = []
    for source in np.ndindex(*SIZES):
        there = dest(*source)
        pairs.append(
            (int(np.ravel_multi_index(source, SIZES)), int(np.ravel_multi_index(there, SIZES)))
        )
    return lax.ppermute(value, AXES, pairs)


def to_owner(value):
    return permute(value, lambda zh, x, a, b, y, c: (a, x, zh, b, y, c))


def over_a(value):
    return permute(value, lambda zh, x, a, b, y, c: (zh, x, 1 - a, b, y, c))


def over_b(value, k):
    return permute(value, lambda zh, x, a, b, y, c: (zh, x, a, b ^ k, y, c))


def over_y(value, k):
    return permute(value, lambda zh, x, a, b, y, c: (zh, x, a, b, y ^ k, c))


def over_c(value):
    return permute(value, lambda zh, x, a, b, y, c: (zh, x, a, b, y, 1 - c))


def over_x(value, k):
    return permute(value, lambda zh, x, a, b, y, c: (zh, x ^ k, a, b, y, c))


def over_zh(value):
    return permute(value, lambda zh, x, a, b, y, c: (1 - zh, x, a, b, y, c))


def member_mask(rows, cols, trials, rank):
    row = lax.broadcasted_iota(jnp.int32, (rows, cols), 0) // trials
    col = lax.broadcasted_iota(jnp.int32, (rows, cols), 1) // rank
    return row == col


def by_trial(values, rows):
    trials, block = values.shape
    trial = lax.broadcasted_iota(jnp.int32, (rows, block), 0) % trials
    out = jnp.broadcast_to(values[:1], (rows, block))
    for j in range(1, trials):
        out = jnp.where(trial == j, jnp.broadcast_to(values[j : j + 1], (rows, block)), out)
    return out


def three_terms(value):
    high = value.astype(jnp.bfloat16).astype(jnp.float32)
    rest = value - high
    middle = rest.astype(jnp.bfloat16).astype(jnp.float32)
    return [high, middle, rest - middle]


def store_packed(out_ref, spikes, factors, trials, rank):
    rows, block = spikes.shape
    full = lax.dot_general(
        spikes, factors, (((1,), (1,)), ((), ())), preferred_element_type=jnp.float32
    )
    kept = jnp.where(member_mask(rows, full.shape[1], trials, rank), full, 0.0)
    trial = lax.broadcasted_iota(jnp.int32, kept.shape, 0) % trials
    parts = [
        jnp.sum(jnp.where(trial == j, kept, 0.0), axis=0, keepdims=True) for j in range(trials)
    ]
    terms = three_terms(jnp.concatenate(parts, axis=0))
    pad = jnp.zeros((EXT - 3 * trials, block), jnp.float32)
    out_ref[:rows] = spikes
    out_ref[rows:] = jnp.concatenate([*terms, pad], axis=0).astype(jnp.bfloat16)


def pack_kernel(spikes_ref, factors_ref, out_ref, *, trials, rank):
    members, _, block = spikes_ref.shape
    spikes = spikes_ref[...].reshape(members * trials, block)
    store_packed(out_ref, spikes, factors_ref[...].reshape(members * rank, block), trials, rank)


def pack(spikes, factors):
    members, trials, block = spikes.shape
    rows, rank = members * trials, factors.shape[1]
    whole = pl.BlockSpec(memory_space=pltpu.VMEM)
    return pl.pallas_call(
        functools.partial(pack_kernel, trials=trials, rank=rank),
        out_shape=jax.ShapeDtypeStruct((rows + EXT, block), jnp.bfloat16),
        in_specs=[whole] * 2,
        out_specs=whole,
        compiler_params=pltpu.CompilerParams(vmem_limit_bytes=4 << 20),
        name="pack",
    )(spikes, factors)


def to_column(value, rows, trials):
    shape = (rows, value.shape[1])
    row = lax.broadcasted_iota(jnp.int32, shape, 0)
    kept = row // trials == lax.broadcasted_iota(jnp.int32, shape, 1)
    if value.shape[0] == 1:
        spread = jnp.broadcast_to(value, shape)
    else:
        spread = by_trial(value, rows)
    return jnp.sum(jnp.where(kept, spread, 0.0), axis=1, keepdims=True)


def update_kernel(*refs, step, trials, rank):
    keep_ref, came_ref, packed_ref, v_ref, a_ref, lanes_ref, ids_ref, count_ref = refs[:8]
    u_ref, f_ref, outs = refs[8], refs[9], refs[10:]
    members, _, block = u_ref.shape
    rows = members * trials
    total = keep_ref[:rows] + came_ref[:rows].astype(jnp.float32)
    tail = came_ref[rows:].astype(jnp.float32)
    proj = keep_ref[rows : rows + trials]
    for term in range(3):
        proj = proj + tail[term * trials : (term + 1) * trials]
    mask = member_mask(rows, members * rank, trials, rank)
    spread = jnp.where(mask, by_trial(proj, rows), 0.0).astype(jnp.bfloat16)
    u_rows = u_ref[...].reshape(members * rank, block)
    low = jnp.dot(spread, u_rows, preferred_element_type=jnp.float32)
    current = by_trial(lanes_ref[4 + step * trials : 4 + (step + 1) * trials], rows)
    half_sign = to_column(0.5 - (ids_ref[...] & 1).astype(jnp.float32), rows, trials)
    count = to_column(count_ref[...].astype(jnp.float32), rows, trials)
    drive = total + half_sign * low + current
    decay_mem, decay_adapt = lanes_ref[0:1], lanes_ref[1:2]
    base, adapt = lanes_ref[2:3], lanes_ref[3:4]
    spikes = packed_ref[:rows].astype(jnp.float32)
    v, a = v_ref[...].reshape(rows, block), a_ref[...].reshape(rows, block)
    v_new = decay_mem * v + (1.0 - decay_mem) * drive - spikes * (base + adapt * a)
    v = jnp.where(count > float(step), v_new, v)
    outs[0][...] = v.reshape(outs[0].shape)
    if step + 1 < STEPS:
        a_new = decay_adapt * a + (1.0 - decay_adapt) * spikes
        a = jnp.where(count > float(step), a_new, a)
        fresh = jax.nn.sigmoid(3.0 * (v - base - adapt * a)).astype(jnp.bfloat16)
        f_rows = f_ref[...].reshape(members * rank, block)
        store_packed(outs[1], fresh, f_rows, trials, rank)
        outs[2][...] = a
        if step + 2 == STEPS:
            a_new = decay_adapt * a + (1.0 - decay_adapt) * fresh.astype(jnp.float32)
            a = jnp.where(count > float(step + 1), a_new, a)
            outs[3][...] = a.reshape(outs[3].shape)


def update(keep, came, packed, v, a, lanes, ids, count, factor_u, factor_v, step):
    members, rank, block = factor_u.shape
    trials = count.shape[0]
    rows = jax.ShapeDtypeStruct((members * trials, block), jnp.float32)
    final = jax.ShapeDtypeStruct((members, trials, block), jnp.float32)
    if step + 1 < STEPS:
        outs = [rows, jax.ShapeDtypeStruct(packed.shape, packed.dtype), rows]
        outs += [final] if step + 2 == STEPS else []
    else:
        outs = [final]
    whole = pl.BlockSpec(memory_space=pltpu.VMEM)
    return pl.pallas_call(
        functools.partial(update_kernel, step=step, trials=trials, rank=rank),
        out_shape=tuple(outs),
        in_specs=[whole] * 10,
        out_specs=(whole,) * len(outs),
        compiler_params=pltpu.CompilerParams(vmem_limit_bytes=6 << 20),
        name="update",
    )(keep, came, packed, v, a, lanes, ids, count, factor_u, factor_v)


def mix_kernel(at_ref, *refs, pieces, rows, trials, late):
    spikes, weights = refs[: 4 * pieces], refs[4 * pieces : 4 * pieces + 4]
    mine_ref, theirs_ref = refs[-2:]
    before = refs[-4:-2]
    flip, shift, y = at_ref[0], at_ref[1], at_ref[2]
    tall, block = spikes[0].shape[1:]
    depth = spikes[0].shape[0] // 2
    extra = None
    for ref in spikes:
        for pair in range(depth):
            tail = ref[2 * pair : 2 * pair + 2, rows:, :].astype(jnp.float32)
            extra = tail if extra is None else extra + tail
    part = extra[:, :trials] + extra[:, trials : 2 * trials] + extra[:, 2 * trials : 3 * trials]

    def run(there):
        total = None
        for q in range(4):
            for high in range(2):
                ref = spikes[q + 4 * high] if pieces == 2 else spikes[q]
                chunk = ref[...] if pieces == 2 else ref[2 * high : 2 * high + 2]
                piece = jnp.dot(
                    chunk.reshape(2 * tall, block),
                    weights[there ^ (2 * high + int(late))][y ^ q],
                    preferred_element_type=jnp.float32,
                )
                total = piece if total is None else total + piece
        for s in range(2):
            for half, ref in enumerate((mine_ref, theirs_ref)):
                value = total[s * tall : (s + 1) * tall, half * block : (half + 1) * block]
                other = part[s]
                if late:
                    value = value + before[half][s ^ flip]
                    other = other + before[half][s ^ flip, rows : rows + trials, :]
                ref[s ^ flip] = value
                ref[s ^ flip, rows : rows + trials, :] = other

    for there in range(4):
        pl.when(shift == there)(functools.partial(run, there))


def mix(at, spikes, weights, rows, trials, before=()):
    _, tall, block = spikes[0].shape
    out = jax.ShapeDtypeStruct((2, tall, block), jnp.float32)
    whole = pl.BlockSpec(memory_space=pltpu.VMEM)
    inputs = len(spikes) * spikes[0].size + 2 * weights[0].size
    return pl.pallas_call(
        functools.partial(
            mix_kernel, pieces=len(spikes) // 4, rows=rows, trials=trials, late=len(before) > 0
        ),
        out_shape=(out, out),
        in_specs=[pl.BlockSpec(memory_space=pltpu.SMEM)]
        + [whole] * (len(spikes) + 4 + len(before)),
        out_specs=(whole, whole),
        cost_estimate=pl.CostEstimate(
            flops=16 * tall * weights[0].size // 2,
            bytes_accessed=2 * inputs + 16 * tall * block,
            transcendentals=0,
        ),
        compiler_params=pltpu.CompilerParams(vmem_limit_bytes=12 << 20),
        name="mix_late" if before else "mix_early",
    )(at, *spikes, *weights, *before)


def fold_kernel(mine_ref, theirs_ref, keep_ref, give_ref, *, rows, trials):
    keep_ref[...] = mine_ref[0] + theirs_ref[0]
    give = mine_ref[1] + theirs_ref[1]
    terms = three_terms(give[rows : rows + trials])
    pad = jnp.zeros((EXT - 3 * trials, give.shape[1]), jnp.float32)
    give_ref[...] = jnp.concatenate([give[:rows], *terms, pad], axis=0).astype(jnp.bfloat16)


def fold(mine, theirs, rows, trials):
    shape = mine.shape[1:]
    whole = pl.BlockSpec(memory_space=pltpu.VMEM)
    return pl.pallas_call(
        functools.partial(fold_kernel, rows=rows, trials=trials),
        out_shape=(
            jax.ShapeDtypeStruct(shape, jnp.float32),
            jax.ShapeDtypeStruct(shape, jnp.bfloat16),
        ),
        in_specs=[whole, whole],
        out_specs=(whole, whole),
        compiler_params=pltpu.CompilerParams(vmem_limit_bytes=4 << 20),
        name="fold",
    )(mine, theirs)


def spread_weights(base_weight, at):
    outs, depth = base_weight.shape
    block = depth // 8
    split = base_weight.reshape(outs, 4, 2, block)
    one = at["c"] == 1
    keep = jnp.where(one, split[:, :, 1], split[:, :, 0]).transpose(1, 2, 0)
    give = jnp.where(one, split[:, :, 0], split[:, :, 1]).transpose(1, 2, 0)
    got = over_c(give)
    own = jnp.concatenate([keep, got], axis=2)
    chunks = [own]
    for k in (1, 2, 3):
        chunks.append(over_x(own, k))
    return chunks


def body(
    v_init,
    a_init,
    z_init,
    base_weight,
    factor_u,
    factor_v,
    in_weight,
    spikes_in,
    step_count,
    member_ids,
    decay_mem,
    decay_adapt,
    thr_base,
    thr_adapt,
):
    members, trials, _ = v_init.shape
    rows = members * trials
    at = {name: lax.axis_index(name) for name in AXES}
    ids = member_ids.reshape(1, members)
    count = step_count.T
    current = jnp.dot(
        spikes_in.reshape(STEPS * trials, -1).astype(jnp.bfloat16),
        in_weight,
        preferred_element_type=jnp.float32,
    )
    lanes = jnp.stack([decay_mem, decay_adapt, thr_base, thr_adapt])
    lanes = jnp.concatenate([lanes, current], axis=0)
    place = jnp.stack([at["a"] ^ at["zh"], at["b"] ^ at["x"], at["y"]])
    v, a = v_init, a_init
    packed = pack(z_init, factor_v)
    weights = spread_weights(base_weight, at)
    for step in range(STEPS):
        held = to_owner(packed)[None]
        other = over_a(held)
        first = [jnp.concatenate([held, other], axis=0)]
        second = [over_b(first[0], 2)]
        held = jnp.concatenate([first[0], second[0]], axis=0)
        if step == 0:
            held, place, lanes = lax.optimization_barrier((held, place, lanes))
        last = [over_b(held, 1)]
        early, came = [held], {}
        for k in (3, 1):
            came[k] = over_y(held, k)
        came[2] = over_y(came[3], 1)
        early += [came[k] for k in (1, 2, 3)]
        for k in (1, 2, 3):
            last.append(over_y(last[0], k))
        halves = mix(place, early, weights, rows, trials)
        mine, theirs = mix(place, last, weights, rows, trials, halves)
        theirs = over_c(theirs)
        keep, give = fold(mine, theirs, rows, trials)
        came = over_zh(give)
        v, *rest = update(
            keep, came, packed, v, a, lanes, ids, count, factor_u, factor_v, step
        )
        if rest:
            packed, a, *ends = rest
            a_out = ends[0] if ends else None
    return (v, a_out)


def solution(mesh):
    fine = Mesh(mesh.devices.reshape(SIZES), AXES)
    in_specs = (
        P(POP, None, BLK),
        P(POP, None, BLK),
        P(POP, None, BLK),
        P(BLK, POP),
        P(POP, None, BLK),
        P(POP, None, BLK),
        P(None, BLK),
        P(),
        P(POP, None),
        P(POP),
        P(BLK),
        P(BLK),
        P(BLK),
        P(BLK),
    )
    out_specs = (P(POP, None, BLK), P(POP, None, BLK))
    return jax.shard_map(body, mesh=fine, in_specs=in_specs, out_specs=out_specs, check_vma=False)
```
